256 devices in a mesh: loop: 32 (over z, x_lo, core), own: 8 (over x_hi, y).
Axes of the slice: x: 4 (x_hi: 2, x_lo: 2; x = x_hi * 2 + x_lo), y: 4, z: 8, core: 2. Of those that a mesh axis runs over, the one named last changes fastest.
Arguments:
- factor_start: float32 [8192, 128], P(('loop', 'own')), may hold values from -6 to 6
- activity: float32 [8192], P(('loop', 'own')), may hold values from 0.05 to 2
- word_factors: bfloat16 [32, 8, 128, 128], P('loop'), may hold values from -0.03125 to 0.03125
- sub_factors: bfloat16 [2048, 128], replicated, may hold values from -6 to 6
- ratings: bfloat16 [32, 8, 32, 8, 128, 128], P('loop', 'own'), may hold values from -6 to 6
- user_tile: int32 [32, 8, 32, 8], P('loop', 'own'), may hold values from 0 to 1
- word_tile: int32 [32, 8, 32, 8], P('loop', 'own'), may hold values from 0 to 7
- subreddit: int32 [32, 8, 32, 8], P('loop', 'own'), may hold values from 0 to 2047
- counts: int32 [32, 8, 32], P('loop', 'own'), may hold values from 1 to 8
- runs: int32 [32, 8, 32, 8, 2, 128], P('loop', 'own'), may hold values from 0 to 128, as said below
Outputs:
- solution: float32 [8192, 128], P(('loop', 'own'))
- residual: float32 [8192, 128], P(('loop', 'own'))
The draws below stay inside these ranges and needn't reach their ends.
Inputs may be any that keep to these rules, and one draw needn't show every extreme that they name: runs[..., 0, a] is the first observed column of row a of a block and runs[..., 1, a] the number of observed columns, counted cyclically from it; each block has a row observed in full.
All inputs are finite; a program needn't handle non-finite values.
Results may differ from the reference program's by a relative error of at most 0.03.
Values may be sent and summed in bfloat16 or wider, within the bound.
A program may use at most 128 MiB of HBM per device.

```python
import math
import jax
import jax.numpy as jnp
from jax import lax

R = 128
TILE = 128
UT = 2
SLOTS = 8
WB = 8
SUBS = 2048
ITERS = 2
U_TOT = 8192
OBS = 37152
N_LOOP = 32
N_OWN = 8


def draw_runs(key, part):
    shape = (N_LOOP, N_OWN, N_LOOP, SLOTS, TILE)
    key_start, key_len, key_pick = jax.random.split(key, 3)
    starts = jax.random.randint(key_start, shape, 0, TILE, dtype=jnp.int32)
    lengths = jax.random.randint(key_len, shape, 1, TILE + 1, dtype=jnp.int32)
    chosen = jax.random.randint(key_pick, shape[:-1] + (1,), 0, TILE, dtype=jnp.int32)
    full_row = jnp.arange(TILE, dtype=jnp.int32) == chosen
    lengths = jnp.where(full_row, TILE, lengths)
    starts = jnp.where(full_row, 0, starts)
    return jnp.stack([starts, lengths], axis=-2).astype(jnp.int32)


def with_ends(values, rng, smallest, largest):
    longest = values.shape.index(max(values.shape))
    spots = []
    for shift in (0, 1):
        where = [jax.random.randint(jax.random.fold_in(rng, axis), (), 0, length) for axis, length in enumerate(values.shape)]
        where[longest] = (where[longest] + shift) % values.shape[longest]
        spots.append(tuple(where))
    return values.at[spots[0]].set(smallest).at[spots[1]].set(largest)


def raised(drawn, rng, source, target, blocks, factor):
    owner, partner = [(jnp.arange(drawn.shape[dim]) // (drawn.shape[dim] // blocks)).reshape([-1 if axis == dim else 1 for axis in range(drawn.ndim)]) for dim in (source, target)]
    chosen = jax.random.permutation(rng, blocks)[partner]
    strong = (owner == chosen) | (owner == (partner + blocks // 2) % blocks)
    return jnp.where(strong, factor * drawn, drawn)


def block_scale(own_key, dims, shards, smallest, top_value):
    level = 1.0
    for axis_at, shards_of in shards:
        heights = jax.random.uniform(jax.random.fold_in(jax.random.fold_in(own_key, 6), axis_at), (shards_of,), jnp.float32, smallest / len(shards), top_value / len(shards))
        level = level * jnp.repeat(jnp.exp(heights), dims[axis_at] // shards_of).reshape((-1,) + (1,) * (len(dims) - 1 - axis_at))
    return level


def normal_values(rng, extent, deviation, most, cuts=(), held_as=jnp.bfloat16):
    drawn = jax.random.normal(rng, extent, jnp.float32) * deviation
    if len(cuts) > 0:
        drawn = block_scale(rng, extent, cuts, -0.22, 0.18) * drawn
    return jnp.clip(drawn, min=-most, max=most).astype(held_as)


def bell_draw_with(key, extent, spread, reach, cuts, heavy, held_as=jnp.bfloat16):
    values = spread * jax.random.normal(key, extent, jnp.float32)
    if cuts:
        values = values * block_scale(key, extent, cuts, -0.22, 0.18)
    return jnp.clip(raised(values, jax.random.fold_in(key, 3), *heavy), -reach, reach).astype(held_as)


def setup_inputs(seed: int = 0) -> dict:
    splits = jax.random.split(jax.random.key(seed), 11)
    return {
        "factor_start": normal_values(splits[0], (U_TOT, R), 1.0, 6.0, ((0, 256),), jnp.float32),
        "activity": jnp.clip(jnp.exp(math.log(2.0) - 3.6888794 * jax.random.uniform(splits[1], (U_TOT,), jnp.float32) ** block_scale(splits[1], (U_TOT,), ((0, 256),), -0.2, 0.2)), 0.05, 2.0),
        "word_factors": normal_values(splits[2], (N_LOOP, WB, TILE, R), OBS ** -0.5, 0.03125, ((0, 32),)),
        "sub_factors": normal_values(splits[3], (SUBS, R), 1.0, 6.0),
        "ratings": bell_draw_with(splits[4], (N_LOOP, N_OWN, N_LOOP, SLOTS, TILE, TILE), 1.0, 6.0, ((0, 32), (1, 8)), (0, 2, 32, 2.75)),
        "user_tile": with_ends(jax.random.randint(splits[5], (N_LOOP, N_OWN, N_LOOP, SLOTS), 0, UT), jax.random.fold_in(splits[5], 1), 0, UT - 1).astype(jnp.int32),
        "word_tile": with_ends(jax.random.randint(splits[6], (N_LOOP, N_OWN, N_LOOP, SLOTS), 0, WB), jax.random.fold_in(splits[6], 1), 0, WB - 1).astype(jnp.int32),
        "subreddit": with_ends(jax.random.randint(splits[7], (N_LOOP, N_OWN, N_LOOP, SLOTS), 0, SUBS), jax.random.fold_in(splits[7], 1), 0, SUBS - 1).astype(jnp.int32),
        "counts": with_ends(jax.random.randint(splits[8], (N_LOOP, N_OWN, N_LOOP), 1, SLOTS + 1), jax.random.fold_in(splits[8], 1), 1, SLOTS).astype(jnp.int32),
        "runs": draw_runs(jax.random.fold_in(splits[10], 71), 0),
    }


ridge = 0.05


def reference(factor_start, activity, word_factors, sub_factors, ratings, user_tile, word_tile, subreddit, counts, runs):
    def data_part(vector, with_values):
        rounded = vector.astype(jnp.bfloat16)
        rounded = lax.optimization_barrier(rounded)
        halves = rounded.astype(jnp.float32).reshape(N_LOOP, UT, TILE, R)

        def one_shard(running, shard):
            word_rows = word_factors[shard][word_tile[shard]]
            sub_rows = sub_factors[subreddit[shard]]
            products = (word_rows.astype(jnp.float32) * sub_rows[..., None, :].astype(jnp.float32)).astype(jnp.bfloat16)
            products = lax.optimization_barrier(products).astype(jnp.float32)
            slot_live = jnp.arange(SLOTS).astype(jnp.int32)[None, None, :] < counts[shard][..., None]
            first_col = runs[shard][..., 0, :]
            run_len = runs[shard][..., 1, :]
            columns = jnp.arange(TILE).astype(jnp.int32)
            observed = (((columns[None, None, None, None, :] - first_col[..., :, None]) % TILE) < run_len[..., :, None]) & slot_live[..., None, None]
            selector = (user_tile[shard][..., None] == jnp.arange(UT).astype(jnp.int32)).astype(jnp.float32)
            picked = jnp.einsum('ogsu,guar->ogsar', selector, halves)
            scores = jnp.einsum('ogsar,ogscr->ogsac', picked, products)
            if with_values:
                scores = ratings[shard].astype(jnp.float32) - scores
            weights = jnp.where(observed, scores, 0.0).astype(jnp.bfloat16)
            weights = lax.optimization_barrier(weights).astype(jnp.float32)
            rows_out = jnp.einsum('ogsac,ogscr->ogsar', weights, products)
            return running + jnp.einsum('ogsu,ogsar->guar', selector, rows_out), None

        start_sum = jnp.zeros((N_LOOP, UT, TILE, R), jnp.float32)
        result, unused = lax.scan(one_shard, start_sum, jnp.arange(N_LOOP).astype(jnp.int32))
        return result.reshape(N_LOOP * UT * TILE, R)

    weight_rows = activity[:, None]
    solution = factor_start
    residual = weight_rows * data_part(solution, True) - ridge * solution
    direction = residual
    norm_now = jnp.sum(residual * residual)
    for iteration in range(ITERS):
        image = weight_rows * data_part(direction, False) + ridge * direction
        step_size = norm_now / jnp.sum(direction * image)
        solution = solution + step_size * direction
        residual = residual - step_size * image
        if iteration + 1 < ITERS:
            norm_next = jnp.sum(residual * residual)
            direction = residual + (norm_next / norm_now) * direction
            norm_now = norm_next
    return solution, residual
```

```python
import functools

import jax
import jax.numpy as jnp
from jax import lax
from jax.experimental import pallas as pl
from jax.experimental.pallas import tpu as pltpu
from jax.sharding import PartitionSpec as P

TILE = 128
R = 128
UT = 2
SLOTS = 8
GROUPS = 32
WB = 8
NP = 4
NQ = 4
NZ = 8
ROWS = 32
STEP_GROUPS = 4
RIDGE = 0.05
MESH = pl.DeviceIdType.MESH
F32 = jnp.float32
BF16 = jnp.bfloat16
VMEM = pl.BlockSpec(memory_space=pltpu.VMEM)


def place():
    loop = lax.axis_index("loop")
    own = lax.axis_index("own")
    c = loop % 2
    x = (own // 4) * 2 + (loop // 2) % 2
    y = own % 4
    z = loop // 4
    return c, x * (1 - c) + y * c, y * (1 - c) + x * c, z


def device(c, p, q, z):
    x = p * (1 - c) + q * c
    y = q * (1 - c) + p * c
    return {"loop": (z * 2 + x % 2) * 2 + c, "own": (x // 2) * 4 + y}


def send(src, dst, sems, k, to):
    copy = pltpu.make_async_remote_copy(
        src_ref=src,
        dst_ref=dst,
        send_sem=sems.at[0, k],
        recv_sem=sems.at[1, k],
        device_id=to,
        device_id_type=MESH,
    )
    copy.start()
    return copy


def enter(here):
    c, p, q, z = here
    barrier = pltpu.get_barrier_semaphore()
    partners = [device(1 - c, q, p, z)]
    partners += [device(c, (p + k) % NP, q, z) for k in range(1, NP)]
    partners += [device(c, p, (q + k) % NQ, z) for k in range(1, NQ)]
    partners += [device(c, p, q, (z + k) % NZ) for k in range(1, NZ)]
    for partner in partners:
        pl.semaphore_signal(barrier, inc=1, device_id=partner, device_id_type=MESH)
    pl.semaphore_wait(barrier, len(partners))


def reduce_scatter(here, part, core_in, p_out, p_in, q_out, q_in, z_out, z_in, c_sem, p_sem, q_sem, z_sem):
    c, p, q, z = here
    copies = []
    core = {}
    for k in (1, 2, 3, 0):
        pp = (q + k) % NP
        core[k] = send(part.at[1 - c, pp], core_in.at[pp], c_sem, k, device(1 - c, q, p, z))
        copies.append(core[k])
    ring = {}
    for k in range(1, NP):
        pp = (p + k) % NP
        core[k].wait_recv()

        def to_send(i, carry):
            p_out[k - 1, i] = (part[c, pp, i] + core_in[pp, i]).astype(BF16)
            return carry

        lax.fori_loop(0, NQ, to_send, 0)
        ring[k] = send(p_out.at[k - 1], p_in.at[k - 1], p_sem, k, device(c, pp, q, z))
        copies.append(ring[k])
    core[0].wait_recv()
    for k in range(1, NP):
        ring[k].wait_recv()

    def chunk(qq):
        total = part[c, p, qq] + core_in[p, qq]
        for k in range(1, NP):
            total = total + p_in[k - 1, qq].astype(F32)
        return total

    ring = {}
    for k in range(1, NQ):
        qq = (q + k) % NQ
        q_out[k - 1] = chunk(qq).astype(BF16)
        ring[k] = send(q_out.at[k - 1], q_in.at[k - 1], q_sem, k, device(c, p, qq, z))
        copies.append(ring[k])
    total = chunk(q)
    for k in range(1, NQ):
        ring[k].wait_recv()
        total = total + q_in[k - 1].astype(F32)
    z_out[...] = total
    ring = {}
    for k in range(1, NZ):
        zz = (z + k) % NZ
        ring[k] = send(z_out.at[zz], z_in.at[k - 1], z_sem, k, device(c, p, q, zz))
        copies.append(ring[k])
    rows = z_out[z]
    for k in range(1, NZ):
        ring[k].wait_recv()
        rows = rows + z_in[k - 1]
    for copy in copies:
        copy.wait_send()
    return rows


class Sum:
    def __init__(self, here, refs):
        self.here = here
        self.slots, self.sems = refs
        self.copies = []

    def start(self, stage, tile):
        c, p, q, z = self.here
        slots, sems = self.slots, self.sems
        place_in, to, base = {
            "z": (z, [device(c, p, q, (z + k) % NZ) for k in range(1, NZ)], 0),
            "q": (q, [device(c, p, (q + k) % NQ, z) for k in range(1, NQ)], 8),
            "p": (p, [device(c, (p + k) % NP, q, z) for k in range(1, NP)], 12),
            "c": (c, [device(1 - c, q, p, z)], 16),
        }[stage]
        self.base, self.size = base, len(to) + 1
        mine = slots.at[base + place_in]
        mine[...] = tile
        self.now = [send(mine, mine, sems, base + k, d) for k, d in enumerate(to)]
        self.copies += self.now

    def finish(self):
        for copy in self.now:
            copy.wait_recv()
        total = self.slots[self.base]
        for k in range(1, self.size):
            total = total + self.slots[self.base + k]
        return total

    def close(self):
        for copy in self.copies:
            copy.wait_send()

    def whole(self, tile):
        for stage in ("z", "q", "p", "c"):
            self.start(stage, tile)
            tile = self.finish()
        self.close()
        return tile


def gather(here, rows, out, sems, total=None, tile=None):
    c, p, q, z = here
    c_sem, p_sem, q_sem, z_sem = sems
    copies = []

    def note(stage, value):
        if total is not None:
            total.start(stage, value)

    out[c, p, q, z] = rows.astype(BF16)
    mine = out.at[c, p, q, z]
    ring = [send(mine, mine, z_sem, k, device(c, p, q, (z + k) % NZ)) for k in range(1, NZ)]
    note("z", tile)
    for copy in ring:
        copy.wait_recv()
    copies += ring
    mine = out.at[c, p, q]
    ring = [send(mine, mine, q_sem, k, device(c, p, (q + k) % NQ, z)) for k in range(1, NQ)]
    if total is not None:
        note("q", total.finish())
    for copy in ring:
        copy.wait_recv()
    copies += ring
    mine = out.at[c, p]
    ring = [send(mine, mine, p_sem, k, device(c, (p + k) % NP, q, z)) for k in range(1, NP)]
    copies += ring
    other = device(1 - c, q, p, z)
    core = [send(mine, mine, c_sem, 0, other)]
    if total is not None:
        note("p", total.finish())
    for k, copy in enumerate(ring, 1):
        copy.wait_recv()
        arrived = out.at[c, (p - k + NP) % NP]
        core.append(send(arrived, arrived, c_sem, k, other))
    if total is not None:
        note("c", total.finish())
        tile = total.finish()
        total.close()
    for copy in core:
        copy.wait_recv()
    for copy in copies + core:
        copy.wait_send()
    return tile


def folded(values):
    tile = values[0:8]
    for k in range(1, ROWS // 8):
        tile = tile + values[8 * k : 8 * k + 8]
    return tile


def all_of(tile):
    return jnp.sum(tile, keepdims=True)


SCATTER_SCRATCH = [
    pltpu.VMEM((NP, NQ, NZ, ROWS, R), F32),
    pltpu.VMEM((NP - 1, NQ, NZ, ROWS, R), BF16),
    pltpu.VMEM((NP - 1, NQ, NZ, ROWS, R), BF16),
    pltpu.VMEM((NQ - 1, NZ, ROWS, R), BF16),
    pltpu.VMEM((NQ - 1, NZ, ROWS, R), BF16),
    pltpu.VMEM((NZ, ROWS, R), F32),
    pltpu.VMEM((NZ - 1, ROWS, R), F32),
    pltpu.SemaphoreType.DMA((2, NP)),
    pltpu.SemaphoreType.DMA((2, NP)),
    pltpu.SemaphoreType.DMA((2, NQ)),
    pltpu.SemaphoreType.DMA((2, NZ)),
]
GATHER_SCRATCH = [
    pltpu.SemaphoreType.DMA((2, NP)),
    pltpu.SemaphoreType.DMA((2, NP)),
    pltpu.SemaphoreType.DMA((2, NQ)),
    pltpu.SemaphoreType.DMA((2, NZ)),
]
SUM_SCRATCH = [pltpu.VMEM((18, 8, R), F32), pltpu.SemaphoreType.DMA((2, 17))]
N_S, N_G, N_SUM = len(SCATTER_SCRATCH), len(GATHER_SCRATCH), len(SUM_SCRATCH)

BLOCK = jax.ShapeDtypeStruct((ROWS, R), F32)
SCALAR = jax.ShapeDtypeStruct((8, R), F32)
WHOLE = jax.ShapeDtypeStruct((2, NP, NQ, NZ, ROWS, R), BF16)


def communicate(kernel, number, outs, scratch, *args):
    return pl.pallas_call(
        kernel,
        out_shape=outs,
        in_specs=[VMEM] * len(args),
        out_specs=[VMEM] * len(outs),
        scratch_shapes=scratch,
        compiler_params=pltpu.CompilerParams(collective_id=number, has_side_effects=True),
        name=f"comm{number}",
    )(*args)


def first_kernel(start, out, *scratch):
    here = place()
    enter(here)
    gather(here, start[...], out, scratch)


def residual_kernel(part, start, activity, residual, square, out, *scratch):
    here = place()
    enter(here)
    rows = reduce_scatter(here, part, *scratch[:N_S])
    r = activity[...] * rows - RIDGE * start[...]
    residual[...] = r
    total = Sum(here, scratch[N_S + N_G :])
    square[...] = gather(here, r, out, scratch[N_S : N_S + N_G], total, folded(r * r))


def step_kernel(part, start, activity, residual, square, solution, later, image, new, out, *scratch):
    here = place()
    enter(here)
    rows = reduce_scatter(here, part, *scratch[:N_S])
    r = residual[...]
    q = activity[...] * rows + RIDGE * r
    image[...] = q
    at = N_S + N_G
    along = Sum(here, scratch[at : at + N_SUM]).whole(folded(r * q))
    step = all_of(square[...]) / all_of(along)
    solution[...] = start[...] + step * r
    r = r - step * q
    later[...] = r
    total = Sum(here, scratch[at + N_SUM :])
    new[...] = gather(here, r, out, scratch[N_S:at], total, folded(r * r))


def last_kernel(part, activity, before, residual, square, image, new, solution, out, left, *scratch):
    here = place()
    enter(here)
    rows = reduce_scatter(here, part, *scratch[:N_S])
    r = residual[...]
    rr = all_of(new[...])
    ratio = rr / all_of(square[...])
    d = r + ratio * before[...]
    q = activity[...] * rows + RIDGE * r + ratio * image[...]
    along = Sum(here, scratch[N_S:]).whole(folded(d * q))
    step = rr / all_of(along)
    out[...] = solution[...] + step * d
    left[...] = r - step * q


def blocks_kernel(first, user_tile, word_tile, counts, *refs):
    if first:
        whole, words, subs, runs, ratings, part, mask = refs
    else:
        whole, words, subs, mask, part = refs
    step = pl.program_id(0)
    columns = lax.broadcasted_iota(jnp.int32, (TILE, TILE), 1)

    def group(i, carry):
        g = step * STEP_GROUPS + i
        c, xl, z = g % 2, (g // 2) % 2, g // 4
        by_x, by_y = 32 - 24 * c, 8 + 24 * c
        base = c * 128 + xl * by_x + z
        for u in range(UT):
            for y in range(4):
                part[base + 2 * u * by_x + y * by_y] = jnp.zeros((ROWS, R), F32)
        sub_rows = subs[i]
        if first:
            run = runs[i]

        def half(slots):
            for s in slots:
                b = g * SLOTS + s
                at = base + user_tile[b] * (2 * by_x)
                rows = jnp.concatenate([whole[at + y * by_y] for y in range(4)], axis=0)
                word = words[word_tile[b]].astype(F32)
                products = (word * sub_rows[s : s + 1]).astype(BF16)
                scores = lax.dot_general(rows, products, (((1,), (1,)), ((), ())), preferred_element_type=F32)
                if first:
                    scores = ratings[i, s].astype(F32) - scores
                    seen = ((columns - run[:, 2 * s : 2 * s + 1]) & (TILE - 1)) < run[:, 2 * s + 1 : 2 * s + 2]
                    seen = jnp.where(seen, 1.0, 0.0)
                    mask[i, s] = seen.astype(BF16)
                    weights = (scores * seen).astype(BF16)
                else:
                    weights = scores.astype(BF16) * mask[i, s]
                added = jnp.dot(weights, products, preferred_element_type=F32)
                for y in range(4):
                    part[at + y * by_y] += added[ROWS * y : ROWS * y + ROWS]

        half(range(4))

        @pl.when(counts[g] > 4)
        def _():
            half(range(4, SLOTS))

        return carry

    lax.fori_loop(0, STEP_GROUPS, group, 0)


def block_sums(tables, whole, words, subs, runs=None, ratings=None, mask=None):
    first = mask is None
    flat = (2 * NP * NQ * NZ, ROWS, R)

    def resident(*shape):
        return pl.BlockSpec(shape, lambda i, *_: (0,) * len(shape))

    def streamed(*shape):
        return pl.BlockSpec((STEP_GROUPS,) + shape, lambda i, *_: (i,) + (0,) * len(shape))

    blocks = streamed(SLOTS, TILE, TILE)
    in_specs = [resident(*flat), resident(WB, TILE, R), streamed(SLOTS, R)]
    out_specs = [resident(*flat)]
    out_shape = [jax.ShapeDtypeStruct(flat, F32)]
    if first:
        in_specs += [streamed(TILE, 2 * SLOTS), blocks]
        out_specs += [blocks]
        out_shape += [jax.ShapeDtypeStruct((GROUPS, SLOTS, TILE, TILE), BF16)]
        args = (runs, ratings)
    else:
        in_specs += [blocks]
        args = (mask,)
    result = pl.pallas_call(
        functools.partial(blocks_kernel, first),
        out_shape=out_shape,
        grid_spec=pltpu.PrefetchScalarGridSpec(
            num_scalar_prefetch=len(tables),
            grid=(GROUPS // STEP_GROUPS,),
            in_specs=in_specs,
            out_specs=out_specs,
        ),
        compiler_params=pltpu.CompilerParams(dimension_semantics=("arbitrary",)),
        name="blocks_first" if first else "blocks_next",
    )(*tables, whole.reshape(flat), words, subs, *args)
    part = result[0].reshape(2, NP, NQ, NZ, ROWS, R)
    return (part, result[1]) if first else part


def on_device(
    factor_start,
    activity,
    word_factors,
    sub_factors,
    ratings,
    user_tile,
    word_tile,
    subreddit,
    counts,
    runs,
):
    live = counts[0, 0]
    tables = (user_tile[0, 0].reshape(-1), word_tile[0, 0].reshape(-1), live)
    words = word_factors[0]
    subs = sub_factors[subreddit[0, 0]].astype(F32)
    used = jnp.arange(SLOTS)[None, :] < live[:, None]
    lengths = jnp.where(used[:, :, None], runs[0, 0][:, :, 1, :], 0)
    run = jnp.stack([runs[0, 0][:, :, 0, :], lengths], axis=2)
    run = run.reshape(GROUPS, 2 * SLOTS, TILE).transpose(0, 2, 1)
    scale = jnp.broadcast_to(activity[:, None], (ROWS, R))

    (whole,) = communicate(first_kernel, 0, [WHOLE], GATHER_SCRATCH, factor_start)
    part, mask = block_sums(tables, whole, words, subs, runs=run, ratings=ratings[0, 0])
    scratch = SCATTER_SCRATCH + GATHER_SCRATCH
    residual, square, whole = communicate(
        residual_kernel, 1, [BLOCK, SCALAR, WHOLE], scratch + SUM_SCRATCH, part, factor_start, scale
    )
    part = block_sums(tables, whole, words, subs, mask=mask)
    solution, later, image, new, whole = communicate(
        step_kernel,
        2,
        [BLOCK, BLOCK, BLOCK, SCALAR, WHOLE],
        scratch + SUM_SCRATCH + SUM_SCRATCH,
        part,
        factor_start,
        scale,
        residual,
        square,
    )
    part = block_sums(tables, whole, words, subs, mask=mask)
    return tuple(
        communicate(
            last_kernel,
            3,
            [BLOCK, BLOCK],
            SCATTER_SCRATCH + SUM_SCRATCH,
            part,
            scale,
            residual,
            later,
            square,
            image,
            new,
            solution,
        )
    )


def solution(mesh):
    placed = (
        P(("loop", "own"), None),
        P(("loop", "own")),
        P("loop", None, None, None),
        P(),
        P("loop", "own", None, None, None, None),
        P("loop", "own", None, None),
        P("loop", "own", None, None),
        P("loop", "own", None, None),
        P("loop", "own", None),
        P("loop", "own", None, None, None, None),
    )
    return jax.shard_map(
        on_device,
        mesh=mesh,
        in_specs=placed,
        out_specs=(P(("loop", "own"), None), P(("loop", "own"), None)),
        check_vma=False,
    )
```

```python
import functools

import jax
import jax.numpy as jnp
from jax import lax
from jax.experimental import pallas as pl
from jax.experimental.pallas import tpu as pltpu
from jax.sharding import PartitionSpec as P

TILE = 128
R = 128
UT = 2
SLOTS = 8
GROUPS = 32
WB = 8
NP = 4
NQ = 4
NZ = 8
ROWS = 32
STEP_GROUPS = 4
RIDGE = 0.05
MESH = pl.DeviceIdType.MESH
F32 = jnp.float32
BF16 = jnp.bfloat16
VMEM = pl.BlockSpec(memory_space=pltpu.VMEM)


def place():
    loop = lax.axis_index("loop")
    own = lax.axis_index("own")
    c = loop % 2
    x = (own // 4) * 2 + (loop // 2) % 2
    y = own % 4
    z = loop // 4
    return c, x * (1 - c) + y * c, y * (1 - c) + x * c, z


def device(c, p, q, z):
    x = p * (1 - c) + q * c
    y = q * (1 - c) + p * c
    return {"loop": (z * 2 + x % 2) * 2 + c, "own": (x // 2) * 4 + y}


def send(src, dst, sems, k, to):
    copy = pltpu.make_async_remote_copy(
        src_ref=src,
        dst_ref=dst,
        send_sem=sems.at[0, k],
        recv_sem=sems.at[1, k],
        device_id=to,
        device_id_type=MESH,
    )
    copy.start()
    return copy


def enter(here):
    c, p, q, z = here
    barrier = pltpu.get_barrier_semaphore()
    partners = [device(1 - c, q, p, z)]
    partners += [device(c, (p + k) % NP, q, z) for k in range(1, NP)]
    partners += [device(c, p, (q + k) % NQ, z) for k in range(1, NQ)]
    partners += [device(c, p, q, (z + k) % NZ) for k in range(1, NZ)]
    for partner in partners:
        pl.semaphore_signal(barrier, inc=1, device_id=partner, device_id_type=MESH)
    pl.semaphore_wait(barrier, len(partners))


def reduce_scatter(here, part, core_in, p_out, p_in, q_out, q_in, z_out, z_in, c_sem, p_sem, q_sem, z_sem):
    c, p, q, z = here
    copies = []
    core = {}
    for k in (1, 2, 3, 0):
        pp = (q + k) % NP
        core[k] = send(part.at[1 - c, pp], core_in.at[pp], c_sem, k, device(1 - c, q, p, z))
        copies.append(core[k])
    ring = {}
    for k in range(1, NP):
        pp = (p + k) % NP
        core[k].wait_recv()

        def to_send(i, carry):
            p_out[k - 1, i] = (part[c, pp, i] + core_in[pp, i]).astype(BF16)
            return carry

        lax.fori_loop(0, NQ, to_send, 0)
        ring[k] = send(p_out.at[k - 1], p_in.at[k - 1], p_sem, k, device(c, pp, q, z))
        copies.append(ring[k])
    core[0].wait_recv()
    for k in range(1, NP):
        ring[k].wait_recv()

    def chunk(qq):
        total = part[c, p, qq] + core_in[p, qq]
        for k in range(1, NP):
            total = total + p_in[k - 1, qq].astype(F32)
        return total

    ring = {}
    for k in range(1, NQ):
        qq = (q + k) % NQ
        q_out[k - 1] = chunk(qq).astype(BF16)
        ring[k] = send(q_out.at[k - 1], q_in.at[k - 1], q_sem, k, device(c, p, qq, z))
        copies.append(ring[k])
    total = chunk(q)
    for k in range(1, NQ):
        ring[k].wait_recv()
        total = total + q_in[k - 1].astype(F32)
    z_out[...] = total
    ring = {}
    for k in range(1, NZ):
        zz = (z + k) % NZ
        ring[k] = send(z_out.at[zz], z_in.at[k - 1], z_sem, k, device(c, p, q, zz))
        copies.append(ring[k])
    rows = z_out[z]
    for k in range(1, NZ):
        ring[k].wait_recv()
        rows = rows + z_in[k - 1]
    for copy in copies:
        copy.wait_send()
    return rows


class Sum:
    def __init__(self, here, refs):
        self.here = here
        self.slots, self.sems = refs
        self.copies = []

    def start(self, stage, tile):
        c, p, q, z = self.here
        slots, sems = self.slots, self.sems
        place_in, to, base = {
            "z": (z, [device(c, p, q, (z + k) % NZ) for k in range(1, NZ)], 0),
            "q": (q, [device(c, p, (q + k) % NQ, z) for k in range(1, NQ)], 8),
            "p": (p, [device(c, (p + k) % NP, q, z) for k in range(1, NP)], 12),
            "c": (c, [device(1 - c, q, p, z)], 16),
        }[stage]
        self.base, self.size = base, len(to) + 1
        mine = slots.at[base + place_in]
        mine[...] = tile
        self.now = [send(mine, mine, sems, base + k, d) for k, d in enumerate(to)]
        self.copies += self.now

    def finish(self):
        for copy in self.now:
            copy.wait_recv()
        total = self.slots[self.base]
        for k in range(1, self.size):
            total = total + self.slots[self.base + k]
        return total

    def close(self):
        for copy in self.copies:
            copy.wait_send()

    def whole(self, tile):
        for stage in ("z", "q", "p", "c"):
            self.start(stage, tile)
            tile = self.finish()
        self.close()
        return tile


def gather(here, rows, out, sems, total=None, tile=None):
    c, p, q, z = here
    c_sem, p_sem, q_sem, z_sem = sems
    copies = []

    def note(stage, value):
        if total is not None:
            total.start(stage, value)

    out[c, p, q, z] = rows.astype(BF16)
    mine = out.at[c, p, q, z]
    ring = [send(mine, mine, z_sem, k, device(c, p, q, (z + k) % NZ)) for k in range(1, NZ)]
    note("z", tile)
    for copy in ring:
        copy.wait_recv()
    copies += ring
    mine = out.at[c, p, q]
    ring = [send(mine, mine, q_sem, k, device(c, p, (q + k) % NQ, z)) for k in range(1, NQ)]
    if total is not None:
        note("q", total.finish())
    for copy in ring:
        copy.wait_recv()
    copies += ring
    mine = out.at[c, p]
    ring = [send(mine, mine, p_sem, k, device(c, (p + k) % NP, q, z)) for k in range(1, NP)]
    copies += ring
    other = device(1 - c, q, p, z)
    core = [send(mine, mine, c_sem, 0, other)]
    if total is not None:
        note("p", total.finish())
    for k, copy in enumerate(ring, 1):
        copy.wait_recv()
        arrived = out.at[c, (p - k + NP) % NP]
        core.append(send(arrived, arrived, c_sem, k, other))
    if total is not None:
        note("c", total.finish())
        tile = total.finish()
        total.close()
    for copy in core:
        copy.wait_recv()
    for copy in copies + core:
        copy.wait_send()
    return tile


def folded(values):
    tile = values[0:8]
    for k in range(1, ROWS // 8):
        tile = tile + values[8 * k : 8 * k + 8]
    return tile


def all_of(tile):
    return jnp.sum(tile, keepdims=True)


SCATTER_SCRATCH = [
    pltpu.VMEM((NP, NQ, NZ, ROWS, R), F32),
    pltpu.VMEM((NP - 1, NQ, NZ, ROWS, R), BF16),
    pltpu.VMEM((NP - 1, NQ, NZ, ROWS, R), BF16),
    pltpu.VMEM((NQ - 1, NZ, ROWS, R), BF16),
    pltpu.VMEM((NQ - 1, NZ, ROWS, R), BF16),
    pltpu.VMEM((NZ, ROWS, R), F32),
    pltpu.VMEM((NZ - 1, ROWS, R), F32),
    pltpu.SemaphoreType.DMA((2, NP)),
    pltpu.SemaphoreType.DMA((2, NP)),
    pltpu.SemaphoreType.DMA((2, NQ)),
    pltpu.SemaphoreType.DMA((2, NZ)),
]
GATHER_SCRATCH = [
    pltpu.SemaphoreType.DMA((2, NP)),
    pltpu.SemaphoreType.DMA((2, NP)),
    pltpu.SemaphoreType.DMA((2, NQ)),
    pltpu.SemaphoreType.DMA((2, NZ)),
]
SUM_SCRATCH = [pltpu.VMEM((18, 8, R), F32), pltpu.SemaphoreType.DMA((2, 17))]
N_S, N_G, N_SUM = len(SCATTER_SCRATCH), len(GATHER_SCRATCH), len(SUM_SCRATCH)

BLOCK = jax.ShapeDtypeStruct((ROWS, R), F32)
SCALAR = jax.ShapeDtypeStruct((8, R), F32)
WHOLE = jax.ShapeDtypeStruct((2, NP, NQ, NZ, ROWS, R), BF16)


def communicate(kernel, number, outs, scratch, *args):
    return pl.pallas_call(
        kernel,
        out_shape=outs,
        in_specs=[VMEM] * len(args),
        out_specs=[VMEM] * len(outs),
        scratch_shapes=scratch,
        compiler_params=pltpu.CompilerParams(
            collective_id=number, has_side_effects=True, vmem_limit_bytes=18 << 20
        ),
        name=f"comm{number}",
    )(*args)


def first_kernel(start, out, *scratch):
    here = place()
    enter(here)
    gather(here, start[...], out, scratch)


def residual_kernel(part, start, activity, residual, square, out, *scratch):
    here = place()
    enter(here)
    rows = reduce_scatter(here, part, *scratch[:N_S])
    r = activity[...] * rows - RIDGE * start[...]
    residual[...] = r
    total = Sum(here, scratch[N_S + N_G :])
    square[...] = gather(here, r, out, scratch[N_S : N_S + N_G], total, folded(r * r))


def step_kernel(part, start, activity, residual, square, solution, later, image, new, out, *scratch):
    here = place()
    enter(here)
    rows = reduce_scatter(here, part, *scratch[:N_S])
    r = residual[...]
    q = activity[...] * rows + RIDGE * r
    image[...] = q
    at = N_S + N_G
    along = Sum(here, scratch[at : at + N_SUM]).whole(folded(r * q))
    step = all_of(square[...]) / all_of(along)
    solution[...] = start[...] + step * r
    r = r - step * q
    later[...] = r
    total = Sum(here, scratch[at + N_SUM :])
    new[...] = gather(here, r, out, scratch[N_S:at], total, folded(r * r))


def last_kernel(part, activity, before, residual, square, image, new, solution, out, left, *scratch):
    here = place()
    enter(here)
    rows = reduce_scatter(here, part, *scratch[:N_S])
    r = residual[...]
    rr = all_of(new[...])
    ratio = rr / all_of(square[...])
    d = r + ratio * before[...]
    q = activity[...] * rows + RIDGE * r + ratio * image[...]
    along = Sum(here, scratch[N_S:]).whole(folded(d * q))
    step = rr / all_of(along)
    out[...] = solution[...] + step * d
    left[...] = r - step * q


def blocks_kernel(first, user_tile, word_tile, counts, *refs):
    if first:
        whole, words, subs, runs, ratings, part, mask = refs
    else:
        whole, words, subs, mask, part = refs
    step = pl.program_id(0)
    columns = lax.broadcasted_iota(jnp.int32, (TILE, TILE), 1)

    def group(i, carry):
        g = step * STEP_GROUPS + i
        c, xl, z = g % 2, (g // 2) % 2, g // 4
        by_x, by_y = 32 - 24 * c, 8 + 24 * c
        base = c * 128 + xl * by_x + z
        sub_rows = subs[i]
        if first:
            run = runs[i]

        def half(slots):
            work = []
            for s in slots:
                b = g * SLOTS + s
                u = user_tile[b]
                at = base + u * (2 * by_x)
                rows = jnp.concatenate([whole[at + y * by_y] for y in range(4)], axis=0)
                word = words[word_tile[b]].astype(F32)
                products = (word * sub_rows[s : s + 1]).astype(BF16)
                scores = lax.dot_general(rows, products, (((1,), (1,)), ((), ())), preferred_element_type=F32)
                work.append((s, u, products, scores))
            top, low = [], []
            for s, u, products, sc in work:
                if first:
                    sc = ratings[i, s].astype(F32) - sc
                    seen = ((columns - run[:, 2 * s : 2 * s + 1]) & (TILE - 1)) < run[:, 2 * s + 1 : 2 * s + 2]
                    seen = jnp.where(seen, 1.0, 0.0)
                    mask[i, s] = seen.astype(BF16)
                    w = (sc * seen).astype(BF16)
                else:
                    w = sc.astype(BF16) * mask[i, s]
                in_low = jnp.full((TILE, TILE), u, jnp.int32).astype(F32).astype(BF16)
                w1 = w * in_low
                top.append(w - w1)
                low.append(w1)
            both = jnp.concatenate([jnp.concatenate(top, 1), jnp.concatenate(low, 1)], 0)
            prod = jnp.concatenate([w[2] for w in work], 0)
            added = jnp.dot(both, prod, preferred_element_type=F32)
            for u in range(UT):
                for y in range(4):
                    r0 = u * TILE + ROWS * y
                    part[base + 2 * u * by_x + y * by_y] = added[r0 : r0 + ROWS]

        half(range(8))


        return carry

    lax.fori_loop(0, STEP_GROUPS, group, 0)


def block_sums(tables, whole, words, subs, runs=None, ratings=None, mask=None):
    first = mask is None
    flat = (2 * NP * NQ * NZ, ROWS, R)

    def resident(*shape):
        return pl.BlockSpec(shape, lambda i, *_: (0,) * len(shape))

    def streamed(*shape):
        return pl.BlockSpec((STEP_GROUPS,) + shape, lambda i, *_: (i,) + (0,) * len(shape))

    blocks = streamed(SLOTS, TILE, TILE)
    in_specs = [resident(*flat), resident(WB, TILE, R), streamed(SLOTS, R)]
    out_specs = [resident(*flat)]
    out_shape = [jax.ShapeDtypeStruct(flat, F32)]
    if first:
        in_specs += [streamed(TILE, 2 * SLOTS), blocks]
        out_specs += [blocks]
        out_shape += [jax.ShapeDtypeStruct((GROUPS, SLOTS, TILE, TILE), BF16)]
        args = (runs, ratings)
    else:
        in_specs += [blocks]
        args = (mask,)
    result = pl.pallas_call(
        functools.partial(blocks_kernel, first),
        out_shape=out_shape,
        grid_spec=pltpu.PrefetchScalarGridSpec(
            num_scalar_prefetch=len(tables),
            grid=(GROUPS // STEP_GROUPS,),
            in_specs=in_specs,
            out_specs=out_specs,
        ),
        compiler_params=pltpu.CompilerParams(
            dimension_semantics=("arbitrary",), vmem_limit_bytes=28 << 20
        ),
        name="blocks_first" if first else "blocks_next",
    )(*tables, whole.reshape(flat), words, subs, *args)
    part = result[0].reshape(2, NP, NQ, NZ, ROWS, R)
    return (part, result[1]) if first else part


def on_device(
    factor_start,
    activity,
    word_factors,
    sub_factors,
    ratings,
    user_tile,
    word_tile,
    subreddit,
    counts,
    runs,
):
    live = counts[0, 0]
    tables = (user_tile[0, 0].reshape(-1), word_tile[0, 0].reshape(-1), live)
    words = word_factors[0]
    subs = sub_factors[subreddit[0, 0]].astype(F32)
    used = jnp.arange(SLOTS)[None, :] < live[:, None]
    lengths = jnp.where(used[:, :, None], runs[0, 0][:, :, 1, :], 0)
    run = jnp.stack([runs[0, 0][:, :, 0, :], lengths], axis=2)
    run = run.reshape(GROUPS, 2 * SLOTS, TILE).transpose(0, 2, 1)
    scale = jnp.broadcast_to(activity[:, None], (ROWS, R))

    (whole,) = communicate(first_kernel, 0, [WHOLE], GATHER_SCRATCH, factor_start)
    part, mask = block_sums(tables, whole, words, subs, runs=run, ratings=ratings[0, 0])
    scratch = SCATTER_SCRATCH + GATHER_SCRATCH
    residual, square, whole = communicate(
        residual_kernel, 1, [BLOCK, SCALAR, WHOLE], scratch + SUM_SCRATCH, part, factor_start, scale
    )
    part = block_sums(tables, whole, words, subs, mask=mask)
    solution, later, image, new, whole = communicate(
        step_kernel,
        2,
        [BLOCK, BLOCK, BLOCK, SCALAR, WHOLE],
        scratch + SUM_SCRATCH + SUM_SCRATCH,
        part,
        factor_start,
        scale,
        residual,
        square,
    )
    part = block_sums(tables, whole, words, subs, mask=mask)
    return tuple(
        communicate(
            last_kernel,
            3,
            [BLOCK, BLOCK],
            SCATTER_SCRATCH + SUM_SCRATCH,
            part,
            scale,
            residual,
            later,
            square,
            image,
            new,
            solution,
        )
    )


def solution(mesh):
    placed = (
        P(("loop", "own"), None),
        P(("loop", "own")),
        P("loop", None, None, None),
        P(),
        P("loop", "own", None, None, None, None),
        P("loop", "own", None, None),
        P("loop", "own", None, None),
        P("loop", "own", None, None),
        P("loop", "own", None),
        P("loop", "own", None, None, None, None),
    )
    return jax.shard_map(
        on_device,
        mesh=mesh,
        in_specs=placed,
        out_specs=(P(("loop", "own"), None), P(("loop", "own"), None)),
        check_vma=False,
    )
```

```python
import functools

import jax
import jax.numpy as jnp
from jax import lax
from jax.experimental import pallas as pl
from jax.experimental.pallas import tpu as pltpu
from jax.sharding import PartitionSpec as P

TILE = 128
R = 128
UT = 2
SLOTS = 8
GROUPS = 32
WB = 8
NP = 4
NQ = 4
NZ = 8
ROWS = 32
STEP_GROUPS = 4
RIDGE = 0.05
MESH = pl.DeviceIdType.MESH
F32 = jnp.float32
BF16 = jnp.bfloat16
VMEM = pl.BlockSpec(memory_space=pltpu.VMEM)


def place():
    loop = lax.axis_index("loop")
    own = lax.axis_index("own")
    c = loop % 2
    x = (own // 4) * 2 + (loop // 2) % 2
    y = own % 4
    z = loop // 4
    return c, x * (1 - c) + y * c, y * (1 - c) + x * c, z


def device(c, p, q, z):
    x = p * (1 - c) + q * c
    y = q * (1 - c) + p * c
    return {"loop": (z * 2 + x % 2) * 2 + c, "own": (x // 2) * 4 + y}


def send(src, dst, sems, k, to):
    copy = pltpu.make_async_remote_copy(
        src_ref=src,
        dst_ref=dst,
        send_sem=sems.at[0, k],
        recv_sem=sems.at[1, k],
        device_id=to,
        device_id_type=MESH,
    )
    copy.start()
    return copy


def enter(here):
    c, p, q, z = here
    barrier = pltpu.get_barrier_semaphore()
    partners = [device(1 - c, q, p, z)]
    partners += [device(c, (p + k) % NP, q, z) for k in range(1, NP)]
    partners += [device(c, p, (q + k) % NQ, z) for k in range(1, NQ)]
    partners += [device(c, p, q, (z + k) % NZ) for k in range(1, NZ)]
    for partner in partners:
        pl.semaphore_signal(barrier, inc=1, device_id=partner, device_id_type=MESH)
    pl.semaphore_wait(barrier, len(partners))


def reduce_scatter(here, part, scratch):
    core_in, p_out, relay, p_in, q_out, q_in, z_out, z_in, c_sem, p_sem, q_sem, z_sem = scratch
    c, p, q, z = here
    other = device(1 - c, q, p, z)
    up, down = device(c, (p + 1) % NP, q, z), device(c, (p + 3) % NP, q, z)
    copies = []
    core = {}
    for k in (2, 1, 3, 0):
        pp = (q + k) % NP
        core[k] = send(part.at[1 - c, pp], core_in.at[pp], c_sem, k, other)
        copies.append(core[k])

    def fill(slot, k, h, relayed):
        pp = (p + k) % NP

        def body(i, carry):
            value = part[c, pp, 2 * h + i] + core_in[pp, 2 * h + i]
            if relayed:
                value = value + relay[h, i].astype(F32)
            p_out[slot, i] = value.astype(BF16)
            return carry

        lax.fori_loop(0, 2, body, 0)

    core[2].wait_recv()
    fill(0, 2, 0, False)
    far = [send(p_out.at[0], relay.at[0], p_sem, 0, up)]
    fill(1, 2, 1, False)
    far.append(send(p_out.at[1], relay.at[1], p_sem, 1, down))
    core[1].wait_recv()
    fill(2, 1, 1, False)
    near = [send(p_out.at[2], p_in.at[0, 1], p_sem, 2, up)]
    core[3].wait_recv()
    fill(3, 3, 0, False)
    near.append(send(p_out.at[3], p_in.at[1, 0], p_sem, 3, down))
    far[0].wait_recv()
    fill(4, 1, 0, True)
    near.append(send(p_out.at[4], p_in.at[0, 0], p_sem, 4, up))
    far[1].wait_recv()
    fill(5, 3, 1, True)
    near.append(send(p_out.at[5], p_in.at[1, 1], p_sem, 5, down))
    copies += far + near
    core[0].wait_recv()
    for copy in near:
        copy.wait_recv()

    def chunk(qq):
        h, i = qq // 2, qq % 2
        total = part[c, p, qq] + core_in[p, qq]
        return total + p_in[0, h, i].astype(F32) + p_in[1, h, i].astype(F32)

    ring = {}
    for k in (2, 1, 3):
        qq = (q + k) % NQ
        q_out[k - 1] = chunk(qq).astype(BF16)
        ring[k] = send(q_out.at[k - 1], q_in.at[k - 1], q_sem, k, device(c, p, qq, z))
        copies.append(ring[k])
    total = chunk(q)
    for k in (1, 3, 2):
        ring[k].wait_recv()
        total = total + q_in[k - 1].astype(F32)
    z_out[...] = total.astype(BF16)
    ring = {}
    order = (4, 3, 5, 2, 6, 1, 7)
    for k in order:
        zz = (z + k) % NZ
        ring[k] = send(z_out.at[zz], z_in.at[k - 1], z_sem, k, device(c, p, q, zz))
        copies.append(ring[k])
    rows = z_out[z].astype(F32)
    for k in order[::-1]:
        ring[k].wait_recv()
        rows = rows + z_in[k - 1].astype(F32)
    for copy in copies:
        copy.wait_send()
    return rows


class Sum:
    def __init__(self, here, refs):
        self.here = here
        self.slots, self.sems = refs
        self.copies = []

    def start(self, stage, tile):
        c, p, q, z = self.here
        slots, sems = self.slots, self.sems
        place_in, to, base = {
            "z": (z, [device(c, p, q, (z + k) % NZ) for k in range(1, NZ)], 0),
            "q": (q, [device(c, p, (q + k) % NQ, z) for k in range(1, NQ)], 8),
            "p": (p, [device(c, (p + k) % NP, q, z) for k in range(1, NP)], 12),
            "c": (c, [device(1 - c, q, p, z)], 16),
        }[stage]
        self.base, self.size = base, len(to) + 1
        mine = slots.at[base + place_in]
        mine[...] = tile
        self.now = [send(mine, mine, sems, base + k, d) for k, d in enumerate(to)]
        self.copies += self.now

    def finish(self):
        for copy in self.now:
            copy.wait_recv()
        total = self.slots[self.base]
        for k in range(1, self.size):
            total = total + self.slots[self.base + k]
        return total

    def close(self):
        for copy in self.copies:
            copy.wait_send()

    def whole(self, tile):
        for stage in ("z", "q", "p", "c"):
            self.start(stage, tile)
            tile = self.finish()
        self.close()
        return tile


def gather(here, rows, out, sems, total=None, tile=None):
    c, p, q, z = here
    c_sem, p_sem, h_sem, q_sem, z_sem = sems
    other = device(1 - c, q, p, z)
    up, down = device(c, (p + 1) % NP, q, z), device(c, (p + 3) % NP, q, z)
    half = NZ // 2
    copies, core = [], []

    out[c, p, q, z] = rows.astype(BF16)
    mine = out.at[c, p, q, z]
    order = (4, 3, 5, 2, 6, 1, 7)
    ring = [send(mine, mine, z_sem, k, device(c, p, q, (z + k) % NZ)) for k in order]
    if total is not None:
        total.start("z", tile)
    for copy in ring[::-1]:
        copy.wait_recv()
    copies += ring

    def across(ref):
        core.append(send(ref, ref, c_sem, len(core), other))

    direct = []

    def along(j, qq):
        ref = out.at[c, p, qq]
        direct.append((send(ref, ref, p_sem, 2 * j, up), send(ref, ref, p_sem, 2 * j + 1, down)))
        copies.extend(direct[-1])

    halves = []

    def onward(j, qq):
        direct[j][0].wait_recv()
        ref = out.at[c, (p + 3) % NP, qq, pl.ds(0, half)]
        first = send(ref, ref, h_sem, 2 * j, up)
        direct[j][1].wait_recv()
        ref = out.at[c, (p + 1) % NP, qq, pl.ds(half, half)]
        second = send(ref, ref, h_sem, 2 * j + 1, down)
        halves.append((first, second))
        copies.extend(halves[-1])
        across(out.at[c, (p + 3) % NP, qq])
        across(out.at[c, (p + 1) % NP, qq])

    steps = (0, 1, 3, 2)
    mine = out.at[c, p, q]
    ring = {k: send(mine, mine, q_sem, k, device(c, p, (q + k) % NQ, z)) for k in (2, 1, 3)}
    copies += ring.values()
    along(0, q)
    across(mine)
    if total is not None:
        total.start("q", total.finish())
    for j in range(1, NQ):
        qq = (q - steps[j] + NQ) % NQ
        ring[steps[j]].wait_recv()
        along(j, qq)
        across(out.at[c, p, qq])
        onward(j - 1, (q - steps[j - 1] + NQ) % NQ)
    if total is not None:
        total.start("p", total.finish())
    onward(NQ - 1, (q - steps[-1] + NQ) % NQ)
    for j in range(NQ):
        for copy in halves[j]:
            copy.wait_recv()
        across(out.at[c, (p + 2) % NP, (q - steps[j] + NQ) % NQ])
    if total is not None:
        total.start("c", total.finish())
        tile = total.finish()
        total.close()
    for copy in core:
        copy.wait_recv()
    for copy in copies + core:
        copy.wait_send()
    return tile


def folded(values):
    tile = values[0:8]
    for k in range(1, ROWS // 8):
        tile = tile + values[8 * k : 8 * k + 8]
    return tile


def all_of(tile):
    return jnp.sum(tile, keepdims=True)


SCATTER_SCRATCH = [
    pltpu.VMEM((NP, NQ, NZ, ROWS, R), F32),
    pltpu.VMEM((6, 2, NZ, ROWS, R), BF16),
    pltpu.VMEM((2, 2, NZ, ROWS, R), BF16),
    pltpu.VMEM((2, 2, 2, NZ, ROWS, R), BF16),
    pltpu.VMEM((NQ - 1, NZ, ROWS, R), BF16),
    pltpu.VMEM((NQ - 1, NZ, ROWS, R), BF16),
    pltpu.VMEM((NZ, ROWS, R), BF16),
    pltpu.VMEM((NZ - 1, ROWS, R), BF16),
    pltpu.SemaphoreType.DMA((2, NP)),
    pltpu.SemaphoreType.DMA((2, 6)),
    pltpu.SemaphoreType.DMA((2, NQ)),
    pltpu.SemaphoreType.DMA((2, NZ)),
]
GATHER_SCRATCH = [
    pltpu.SemaphoreType.DMA((2, NP * NQ)),
    pltpu.SemaphoreType.DMA((2, 2 * NQ)),
    pltpu.SemaphoreType.DMA((2, 2 * NQ)),
    pltpu.SemaphoreType.DMA((2, NQ)),
    pltpu.SemaphoreType.DMA((2, NZ)),
]
SUM_SCRATCH = [pltpu.VMEM((18, 8, R), F32), pltpu.SemaphoreType.DMA((2, 17))]
N_S, N_G, N_SUM = len(SCATTER_SCRATCH), len(GATHER_SCRATCH), len(SUM_SCRATCH)

BLOCK = jax.ShapeDtypeStruct((ROWS, R), F32)
SCALAR = jax.ShapeDtypeStruct((8, R), F32)
WHOLE = jax.ShapeDtypeStruct((2, NP, NQ, NZ, ROWS, R), BF16)


def communicate(kernel, number, outs, scratch, *args):
    return pl.pallas_call(
        kernel,
        out_shape=outs,
        in_specs=[VMEM] * len(args),
        out_specs=[VMEM] * len(outs),
        scratch_shapes=scratch,
        compiler_params=pltpu.CompilerParams(
            collective_id=number, has_side_effects=True, vmem_limit_bytes=18 << 20
        ),
        name=f"comm{number}",
    )(*args)


def first_kernel(start, out, *scratch):
    here = place()
    enter(here)
    gather(here, start[...], out, scratch)


def residual_kernel(part, start, activity, residual, square, out, *scratch):
    here = place()
    enter(here)
    rows = reduce_scatter(here, part, scratch[:N_S])
    r = activity[...] * rows - RIDGE * start[...]
    residual[...] = r
    total = Sum(here, scratch[N_S + N_G :])
    square[...] = gather(here, r, out, scratch[N_S : N_S + N_G], total, folded(r * r))


def step_kernel(part, start, activity, residual, square, solution, later, image, new, out, *scratch):
    here = place()
    enter(here)
    rows = reduce_scatter(here, part, scratch[:N_S])
    r = residual[...]
    q = activity[...] * rows + RIDGE * r
    image[...] = q
    at = N_S + N_G
    along = Sum(here, scratch[at : at + N_SUM]).whole(folded(r * q))
    step = all_of(square[...]) / all_of(along)
    solution[...] = start[...] + step * r
    r = r - step * q
    later[...] = r
    total = Sum(here, scratch[at + N_SUM :])
    new[...] = gather(here, r, out, scratch[N_S:at], total, folded(r * r))


def last_kernel(part, activity, before, residual, square, image, new, solution, out, left, *scratch):
    here = place()
    enter(here)
    rows = reduce_scatter(here, part, scratch[:N_S])
    r = residual[...]
    rr = all_of(new[...])
    ratio = rr / all_of(square[...])
    d = r + ratio * before[...]
    q = activity[...] * rows + RIDGE * r + ratio * image[...]
    along = Sum(here, scratch[N_S:]).whole(folded(d * q))
    step = rr / all_of(along)
    out[...] = solution[...] + step * d
    left[...] = r - step * q


def blocks_kernel(first, user_tile, word_tile, counts, *refs):
    if first:
        whole, words, subs, runs, ratings, part, mask = refs
    else:
        whole, words, subs, mask, part = refs
    step = pl.program_id(0)
    columns = lax.broadcasted_iota(jnp.int32, (TILE, TILE), 1)

    def group(i, carry):
        g = step * STEP_GROUPS + i
        c, xl, z = g % 2, (g // 2) % 2, g // 4
        by_x, by_y = 32 - 24 * c, 8 + 24 * c
        base = c * 128 + xl * by_x + z
        sub_rows = subs[i]
        if first:
            run = runs[i]

        def half(slots):
            work = []
            for s in slots:
                b = g * SLOTS + s
                u = user_tile[b]
                at = base + u * (2 * by_x)
                rows = jnp.concatenate([whole[at + y * by_y] for y in range(4)], axis=0)
                word = words[word_tile[b]].astype(F32)
                products = (word * sub_rows[s : s + 1]).astype(BF16)
                scores = lax.dot_general(rows, products, (((1,), (1,)), ((), ())), preferred_element_type=F32)
                work.append((s, u, products, scores))
            top, low = [], []
            for s, u, products, sc in work:
                if first:
                    sc = ratings[i, s].astype(F32) - sc
                    seen = ((columns - run[:, 2 * s : 2 * s + 1]) & (TILE - 1)) < run[:, 2 * s + 1 : 2 * s + 2]
                    seen = jnp.where(seen, 1.0, 0.0)
                    mask[i, s] = seen.astype(BF16)
                    w = (sc * seen).astype(BF16)
                else:
                    w = sc.astype(BF16) * mask[i, s]
                in_low = jnp.full((TILE, TILE), u, jnp.int32).astype(F32).astype(BF16)
                w1 = w * in_low
                top.append(w - w1)
                low.append(w1)
            both = jnp.concatenate([jnp.concatenate(top, 1), jnp.concatenate(low, 1)], 0)
            prod = jnp.concatenate([w[2] for w in work], 0)
            added = jnp.dot(both, prod, preferred_element_type=F32)
            for u in range(UT):
                for y in range(4):
                    r0 = u * TILE + ROWS * y
                    part[base + 2 * u * by_x + y * by_y] = added[r0 : r0 + ROWS]

        half(range(8))


        return carry

    lax.fori_loop(0, STEP_GROUPS, group, 0)


def block_sums(tables, whole, words, subs, runs=None, ratings=None, mask=None):
    first = mask is None
    flat = (2 * NP * NQ * NZ, ROWS, R)

    def resident(*shape):
        return pl.BlockSpec(shape, lambda i, *_: (0,) * len(shape))

    def streamed(*shape):
        return pl.BlockSpec((STEP_GROUPS,) + shape, lambda i, *_: (i,) + (0,) * len(shape))

    blocks = streamed(SLOTS, TILE, TILE)
    in_specs = [resident(*flat), resident(WB, TILE, R), streamed(SLOTS, R)]
    out_specs = [resident(*flat)]
    out_shape = [jax.ShapeDtypeStruct(flat, F32)]
    if first:
        in_specs += [streamed(TILE, 2 * SLOTS), blocks]
        out_specs += [blocks]
        out_shape += [jax.ShapeDtypeStruct((GROUPS, SLOTS, TILE, TILE), BF16)]
        args = (runs, ratings)
    else:
        in_specs += [blocks]
        args = (mask,)
    result = pl.pallas_call(
        functools.partial(blocks_kernel, first),
        out_shape=out_shape,
        grid_spec=pltpu.PrefetchScalarGridSpec(
            num_scalar_prefetch=len(tables),
            grid=(GROUPS // STEP_GROUPS,),
            in_specs=in_specs,
            out_specs=out_specs,
        ),
        compiler_params=pltpu.CompilerParams(
            dimension_semantics=("arbitrary",), vmem_limit_bytes=28 << 20
        ),
        name="blocks_first" if first else "blocks_next",
    )(*tables, whole.reshape(flat), words, subs, *args)
    part = result[0].reshape(2, NP, NQ, NZ, ROWS, R)
    return (part, result[1]) if first else part


def on_device(
    factor_start,
    activity,
    word_factors,
    sub_factors,
    ratings,
    user_tile,
    word_tile,
    subreddit,
    counts,
    runs,
):
    live = counts[0, 0]
    tables = (user_tile[0, 0].reshape(-1), word_tile[0, 0].reshape(-1), live)
    words = word_factors[0]
    subs = sub_factors[subreddit[0, 0]].astype(F32)
    used = jnp.arange(SLOTS)[None, :] < live[:, None]
    lengths = jnp.where(used[:, :, None], runs[0, 0][:, :, 1, :], 0)
    run = jnp.stack([runs[0, 0][:, :, 0, :], lengths], axis=2)
    run = run.reshape(GROUPS, 2 * SLOTS, TILE).transpose(0, 2, 1)
    scale = jnp.broadcast_to(activity[:, None], (ROWS, R))

    (whole,) = communicate(first_kernel, 0, [WHOLE], GATHER_SCRATCH, factor_start)
    part, mask = block_sums(tables, whole, words, subs, runs=run, ratings=ratings[0, 0])
    scratch = SCATTER_SCRATCH + GATHER_SCRATCH
    residual, square, whole = communicate(
        residual_kernel, 1, [BLOCK, SCALAR, WHOLE], scratch + SUM_SCRATCH, part, factor_start, scale
    )
    part = block_sums(tables, whole, words, subs, mask=mask)
    solution, later, image, new, whole = communicate(
        step_kernel,
        2,
        [BLOCK, BLOCK, BLOCK, SCALAR, WHOLE],
        scratch + SUM_SCRATCH + SUM_SCRATCH,
        part,
        factor_start,
        scale,
        residual,
        square,
    )
    part = block_sums(tables, whole, words, subs, mask=mask)
    return tuple(
        communicate(
            last_kernel,
            3,
            [BLOCK, BLOCK],
            SCATTER_SCRATCH + SUM_SCRATCH,
            part,
            scale,
            residual,
            later,
            square,
            image,
            new,
            solution,
        )
    )


def solution(mesh):
    placed = (
        P(("loop", "own"), None),
        P(("loop", "own")),
        P("loop", None, None, None),
        P(),
        P("loop", "own", None, None, None, None),
        P("loop", "own", None, None),
        P("loop", "own", None, None),
        P("loop", "own", None, None),
        P("loop", "own", None),
        P("loop", "own", None, None, None, None),
    )
    return jax.shard_map(
        on_device,
        mesh=mesh,
        in_specs=placed,
        out_specs=(P(("loop", "own"), None), P(("loop", "own"), None)),
        check_vma=False,
    )
```

```python
import jax
import jax.numpy as jnp
from jax import lax
from jax.experimental import pallas as pl
from jax.experimental.pallas import tpu as pltpu
from jax.sharding import PartitionSpec as P

TILE = 128
R = 128
UT = 2
SLOTS = 8
GROUPS = 32
NP = 4
NQ = 4
NZ = 8
ROWS = 32
RIDGE = 0.05
MESH = pl.DeviceIdType.MESH
F32 = jnp.float32
BF16 = jnp.bfloat16
VMEM = pl.BlockSpec(memory_space=pltpu.VMEM)


def place():
    loop = lax.axis_index("loop")
    own = lax.axis_index("own")
    c = loop % 2
    x = (own // 4) * 2 + (loop // 2) % 2
    y = own % 4
    z = loop // 4
    return c, x * (1 - c) + y * c, y * (1 - c) + x * c, z


def device(c, p, q, z):
    x = p * (1 - c) + q * c
    y = q * (1 - c) + p * c
    return {"loop": (z * 2 + x % 2) * 2 + c, "own": (x // 2) * 4 + y}


def send(src, dst, sems, k, to):
    copy = pltpu.make_async_remote_copy(
        src_ref=src,
        dst_ref=dst,
        send_sem=sems.at[0, k],
        recv_sem=sems.at[1, k],
        device_id=to,
        device_id_type=MESH,
    )
    copy.start()
    return copy


def enter(here):
    c, p, q, z = here
    barrier = pltpu.get_barrier_semaphore()
    partners = [device(1 - c, q, p, z)]
    partners += [device(c, (p + k) % NP, q, z) for k in range(1, NP)]
    partners += [device(c, p, (q + k) % NQ, z) for k in range(1, NQ)]
    partners += [device(c, p, q, (z + k) % NZ) for k in range(1, NZ)]
    for partner in partners:
        pl.semaphore_signal(barrier, inc=1, device_id=partner, device_id_type=MESH)
    pl.semaphore_wait(barrier, len(partners))


def to_partner(here, part, core_in, c_sem):
    c, p, q, z = here
    core = {}
    for k in (2, 1, 3, 0):
        pp = (q + k) % NP
        core[k] = send(part.at[1 - c, pp], core_in.at[pp], c_sem, k, device(1 - c, q, p, z))
    return core


def reduce_scatter(here, part, core, scratch):
    core_in, p_out, relay, p_in, q_out, q_in, z_out, z_in, p_sem, q_sem, z_sem = scratch
    c, p, q, z = here
    up, down = device(c, (p + 1) % NP, q, z), device(c, (p + 3) % NP, q, z)
    copies = list(core.values())

    def fill(slot, k, h, relayed):
        pp = (p + k) % NP

        def body(i, carry):
            value = part[c, pp, 2 * h + i] + core_in[pp, 2 * h + i]
            if relayed:
                value = value + relay[h, i].astype(F32)
            p_out[slot, i] = value.astype(BF16)
            return carry

        lax.fori_loop(0, 2, body, 0)

    core[2].wait_recv()
    fill(0, 2, 0, False)
    far = [send(p_out.at[0], relay.at[0], p_sem, 0, up)]
    fill(1, 2, 1, False)
    far.append(send(p_out.at[1], relay.at[1], p_sem, 1, down))
    core[1].wait_recv()
    fill(2, 1, 1, False)
    near = [send(p_out.at[2], p_in.at[0, 1], p_sem, 2, up)]
    core[3].wait_recv()
    fill(3, 3, 0, False)
    near.append(send(p_out.at[3], p_in.at[1, 0], p_sem, 3, down))
    far[0].wait_recv()
    fill(4, 1, 0, True)
    near.append(send(p_out.at[4], p_in.at[0, 0], p_sem, 4, up))
    far[1].wait_recv()
    fill(5, 3, 1, True)
    near.append(send(p_out.at[5], p_in.at[1, 1], p_sem, 5, down))
    copies += far + near
    core[0].wait_recv()
    for copy in near:
        copy.wait_recv()

    def chunk(qq):
        h, i = qq // 2, qq % 2
        total = part[c, p, qq] + core_in[p, qq]
        return total + p_in[0, h, i].astype(F32) + p_in[1, h, i].astype(F32)

    ring = {}
    for k in (2, 1, 3):
        qq = (q + k) % NQ
        q_out[k - 1] = chunk(qq).astype(BF16)
        ring[k] = send(q_out.at[k - 1], q_in.at[k - 1], q_sem, k, device(c, p, qq, z))
        copies.append(ring[k])
    total = chunk(q)
    for k in (1, 3, 2):
        ring[k].wait_recv()
        total = total + q_in[k - 1].astype(F32)
    z_out[...] = total.astype(BF16)
    ring = {}
    order = (4, 3, 5, 2, 6, 1, 7)
    for k in order:
        zz = (z + k) % NZ
        ring[k] = send(z_out.at[zz], z_in.at[k - 1], z_sem, k, device(c, p, q, zz))
        copies.append(ring[k])
    rows = z_out[z].astype(F32)
    for k in order[::-1]:
        ring[k].wait_recv()
        rows = rows + z_in[k - 1].astype(F32)
    for copy in copies:
        copy.wait_send()
    return rows


class Sum:
    def __init__(self, here, refs):
        self.here = here
        self.slots, self.sems = refs
        self.copies = []

    def start(self, stage, tile):
        c, p, q, z = self.here
        slots, sems = self.slots, self.sems
        place_in, to, base = {
            "z": (z, [device(c, p, q, (z + k) % NZ) for k in range(1, NZ)], 0),
            "q": (q, [device(c, p, (q + k) % NQ, z) for k in range(1, NQ)], 8),
            "p": (p, [device(c, (p + k) % NP, q, z) for k in range(1, NP)], 12),
            "c": (c, [device(1 - c, q, p, z)], 16),
        }[stage]
        self.base, self.size = base, len(to) + 1
        mine = slots.at[base + place_in]
        mine[...] = tile
        self.now = [send(mine, mine, sems, base + k, d) for k, d in enumerate(to)]
        self.copies += self.now

    def finish(self):
        for copy in self.now:
            copy.wait_recv()
        total = self.slots[self.base]
        for k in range(1, self.size):
            total = total + self.slots[self.base + k]
        return total

    def close(self):
        for copy in self.copies:
            copy.wait_send()

    def whole(self, tile):
        for stage in ("z", "q", "p", "c"):
            self.start(stage, tile)
            tile = self.finish()
        self.close()
        return tile


def gather(here, rows, out, sems, total=None, tile=None, meanwhile=None):
    c, p, q, z = here
    c_sem, p_sem, q_sem, z_sem = sems
    copies = []

    def note(stage, value):
        if total is not None:
            total.start(stage, value)

    out[c, p, q, z] = rows.astype(BF16)
    mine = out.at[c, p, q, z]
    ring = [send(mine, mine, z_sem, k, device(c, p, q, (z + k) % NZ)) for k in (4, 3, 5, 2, 6, 1, 7)]
    note("z", tile)
    if meanwhile is not None:
        meanwhile(0)
    for copy in ring:
        copy.wait_recv()
    copies += ring
    mine = out.at[c, p, q]
    ring = [send(mine, mine, q_sem, k, device(c, p, (q + k) % NQ, z)) for k in range(1, NQ)]
    if total is not None:
        note("q", total.finish())
    if meanwhile is not None:
        meanwhile(1)
    for copy in ring:
        copy.wait_recv()
    copies += ring
    mine = out.at[c, p]
    ring = [send(mine, mine, p_sem, k, device(c, (p + k) % NP, q, z)) for k in range(1, NP)]
    copies += ring
    other = device(1 - c, q, p, z)
    core = [send(mine, mine, c_sem, 0, other)]
    if total is not None:
        note("p", total.finish())
    if meanwhile is not None:
        meanwhile(2)
    for k, copy in enumerate(ring, 1):
        copy.wait_recv()
        arrived = out.at[c, (p - k + NP) % NP]
        core.append(send(arrived, arrived, c_sem, k, other))
    if total is not None:
        note("c", total.finish())
        tile = total.finish()
        total.close()
    for copy in core:
        copy.wait_recv()
    for copy in copies + core:
        copy.wait_send()
    return tile


def folded(values):
    tile = values[0:8]
    for k in range(1, ROWS // 8):
        tile = tile + values[8 * k : 8 * k + 8]
    return tile


def all_of(tile):
    return jnp.sum(tile, keepdims=True)


def masks(run, mask, begin, end):
    columns = lax.broadcasted_iota(jnp.int32, (TILE, TILE), 1)

    def group(g, carry):
        here = run[g]
        for s in range(SLOTS):
            first, length = here[:, 2 * s : 2 * s + 1], here[:, 2 * s + 1 : 2 * s + 2]
            seen = ((columns - first) & (TILE - 1)) < length
            mask[g, s] = jnp.where(seen, 1.0, 0.0).astype(BF16)
        return carry

    lax.fori_loop(begin, end, group, 0)


def block_sums(core, whole, words, subs, user_tile, word_tile, mask, ratings, part):
    def group(n, carry):
        g = 2 * n + core
        xl, z = n % 2, n // 2

        def rows_at(ref, u, y):
            x = 2 * u + xl
            return ref.at[core, x * (1 - core) + y * core, y * (1 - core) + x * core, z]

        sub_rows = subs[g]
        work = []
        for s in range(SLOTS):
            u = user_tile[g * SLOTS + s]
            rows = jnp.concatenate([rows_at(whole, u, y)[...] for y in range(4)], axis=0)
            word = words[word_tile[g * SLOTS + s]].astype(F32)
            products = (word * sub_rows[s : s + 1]).astype(BF16)
            scores = lax.dot_general(rows, products, (((1,), (1,)), ((), ())), preferred_element_type=F32)
            work.append((s, u, products, scores))
        top, low = [], []
        for s, u, products, scores in work:
            if ratings is not None:
                scores = ratings[g, s].astype(F32) - scores
            weights = scores.astype(BF16) * mask[g, s]
            lower = weights * jnp.full((TILE, TILE), u, jnp.int32).astype(F32).astype(BF16)
            top.append(weights - lower)
            low.append(lower)
        both = jnp.concatenate([jnp.concatenate(top, 1), jnp.concatenate(low, 1)], 0)
        products = jnp.concatenate([w[2] for w in work], 0)
        sums = jnp.dot(both, products, preferred_element_type=F32)
        for u in range(UT):
            for y in range(4):
                at = u * TILE + ROWS * y
                rows_at(part, u, y)[...] = sums[at : at + ROWS]
        return carry

    lax.fori_loop(0, GROUPS // 2, group, 0)


DMA = pltpu.SemaphoreType.DMA
SCATTER_SCRATCH = [
    pltpu.VMEM((NP, NQ, NZ, ROWS, R), F32),
    pltpu.VMEM((6, 2, NZ, ROWS, R), BF16),
    pltpu.VMEM((2, 2, NZ, ROWS, R), BF16),
    pltpu.VMEM((2, 2, 2, NZ, ROWS, R), BF16),
    pltpu.VMEM((NQ - 1, NZ, ROWS, R), BF16),
    pltpu.VMEM((NQ - 1, NZ, ROWS, R), BF16),
    pltpu.VMEM((NZ, ROWS, R), BF16),
    pltpu.VMEM((NZ - 1, ROWS, R), BF16),
    DMA((2, 6)),
    DMA((2, NQ)),
    DMA((2, NZ)),
]
GATHER_SCRATCH = [DMA((2, NP)), DMA((2, NP)), DMA((2, NQ)), DMA((2, NZ))]
SUM_SCRATCH = [pltpu.VMEM((18, 8, R), F32), DMA((2, 17))]
WHOLE = pltpu.VMEM((2, NP, NQ, NZ, ROWS, R), BF16)
BLOCKS = pltpu.VMEM((GROUPS, SLOTS, TILE, TILE), BF16)
SCRATCH = [WHOLE] * 3 + [pltpu.VMEM((2, NP, NQ, NZ, ROWS, R), F32), BLOCKS, BLOCKS, DMA, DMA((2, NP))]
N_S, N_G, N_SUM, N_OWN = len(SCATTER_SCRATCH), len(GATHER_SCRATCH), len(SUM_SCRATCH), len(SCRATCH)


def step_kernel(start, activity, words, subs, run, user_tile, word_tile, ratings, out, left, *scratch):
    whole0, whole1, whole2, part, mask, held, fetch_sem, core_sem = scratch[:N_OWN]
    scatter = scratch[N_OWN : N_OWN + N_S]
    at = N_OWN + N_S
    gather_sems = scratch[at : at + N_G]
    sums = [scratch[at + N_G + i * N_SUM : at + N_G + (i + 1) * N_SUM] for i in range(4)]
    here = place()
    fetch = pltpu.make_async_copy(ratings, held, fetch_sem)
    fetch.start()
    enter(here)

    def data(whole, values):
        c = here[0]
        block_sums(1 - c, whole, words, subs, user_tile, word_tile, mask, values, part)
        core = to_partner(here, part, scatter[0], core_sem)
        block_sums(c, whole, words, subs, user_tile, word_tile, mask, values, part)
        return activity[...] * reduce_scatter(here, part, core, scatter)

    cuts = (0, 11, 22, GROUPS)
    gather(here, start[...], whole0, gather_sems, meanwhile=lambda i: masks(run, mask, cuts[i], cuts[i + 1]))
    fetch.wait()
    r = data(whole0, held) - RIDGE * start[...]
    rr = all_of(gather(here, r, whole1, gather_sems, Sum(here, sums[0]), folded(r * r)))
    q = data(whole1, None) + RIDGE * r
    step = rr / all_of(Sum(here, sums[1]).whole(folded(r * q)))
    solution = start[...] + step * r
    later = r - step * q
    new = all_of(gather(here, later, whole2, gather_sems, Sum(here, sums[2]), folded(later * later)))
    ratio = new / rr
    d = later + ratio * r
    q = data(whole2, None) + RIDGE * later + ratio * q
    step = new / all_of(Sum(here, sums[3]).whole(folded(d * q)))
    out[...] = solution + step * d
    left[...] = later - step * q


def on_device(
    factor_start,
    activity,
    word_factors,
    sub_factors,
    ratings,
    user_tile,
    word_tile,
    subreddit,
    counts,
    runs,
):
    live = counts[0, 0]
    subs = sub_factors[subreddit[0, 0]].astype(F32)
    used = jnp.arange(SLOTS)[None, :] < live[:, None]
    lengths = jnp.where(used[:, :, None], runs[0, 0][:, :, 1, :], 0)
    run = jnp.stack([runs[0, 0][:, :, 0, :], lengths], axis=2)
    run = run.reshape(GROUPS, 2 * SLOTS, TILE).transpose(0, 2, 1)
    scale = jnp.broadcast_to(activity[:, None], (ROWS, R))
    table = pl.BlockSpec(memory_space=pltpu.SMEM)
    block = jax.ShapeDtypeStruct((ROWS, R), F32)
    return tuple(
        pl.pallas_call(
            step_kernel,
            out_shape=[block, block],
            in_specs=[VMEM] * 5 + [table] * 2 + [pl.BlockSpec(memory_space=pl.ANY)],
            out_specs=[VMEM] * 2,
            scratch_shapes=SCRATCH + SCATTER_SCRATCH + GATHER_SCRATCH + SUM_SCRATCH * 4,
            compiler_params=pltpu.CompilerParams(
                collective_id=0, has_side_effects=True, vmem_limit_bytes=56 << 20
            ),
            name="step",
        )(
            factor_start,
            scale,
            word_factors[0],
            subs,
            run,
            user_tile[0, 0].reshape(-1),
            word_tile[0, 0].reshape(-1),
            ratings[0, 0],
        )
    )


def solution(mesh):
    placed = (
        P(("loop", "own"), None),
        P(("loop", "own")),
        P("loop", None, None, None),
        P(),
        P("loop", "own", None, None, None, None),
        P("loop", "own", None, None),
        P("loop", "own", None, None),
        P("loop", "own", None, None),
        P("loop", "own", None),
        P("loop", "own", None, None, None, None),
    )
    return jax.shard_map(
        on_device,
        mesh=mesh,
        in_specs=placed,
        out_specs=(P(("loop", "own"), None), P(("loop", "own"), None)),
        check_vma=False,
    )
```

```python
import jax
import jax.numpy as jnp
from jax import lax
from jax.experimental import pallas as pl
from jax.experimental.pallas import tpu as pltpu
from jax.sharding import PartitionSpec as P

TILE = 128
R = 128
UT = 2
SLOTS = 8
SUBS = 2048
GROUPS = 32
NP = 4
NQ = 4
NZ = 8
ROWS = 32
RIDGE = 0.05
MESH = pl.DeviceIdType.MESH
F32 = jnp.float32
BF16 = jnp.bfloat16
VMEM = pl.BlockSpec(memory_space=pltpu.VMEM)


def place():
    loop = lax.axis_index("loop")
    own = lax.axis_index("own")
    c = loop % 2
    x = (own // 4) * 2 + (loop // 2) % 2
    y = own % 4
    z = loop // 4
    return c, x * (1 - c) + y * c, y * (1 - c) + x * c, z


def device(c, p, q, z):
    x = p * (1 - c) + q * c
    y = q * (1 - c) + p * c
    return {"loop": (z * 2 + x % 2) * 2 + c, "own": (x // 2) * 4 + y}


def send(src, dst, sems, k, to):
    copy = pltpu.make_async_remote_copy(
        src_ref=src,
        dst_ref=dst,
        send_sem=sems.at[0, k],
        recv_sem=sems.at[1, k],
        device_id=to,
        device_id_type=MESH,
    )
    copy.start()
    return copy


def enter(here):
    c, p, q, z = here
    barrier = pltpu.get_barrier_semaphore()
    partners = [device(1 - c, q, (p + k) % NQ, z) for k in range(NQ)]
    partners += [device(1 - c, (q + k) % NP, p, z) for k in range(1, NP)]
    partners += [device(c, (p + k) % NP, q, z) for k in range(1, NP)]
    partners += [device(c, p, (q + k) % NQ, z) for k in range(1, NQ)]
    partners += [device(c, p, q, (z + k) % NZ) for k in range(1, NZ)]
    for partner in partners:
        pl.semaphore_signal(barrier, inc=1, device_id=partner, device_id_type=MESH)
    pl.semaphore_wait(barrier, len(partners))


def to_partner(here, part, core_in, c_sem):
    c, p, q, z = here
    core = {}
    for k in (2, 1, 3, 0):
        pp = (q + k) % NP
        core[k] = send(part.at[1 - c, pp], core_in.at[pp], c_sem, k, device(1 - c, q, p, z))
    return core


def reduce_scatter(here, part, core, scratch, total=None, weigh=None, own=None):
    core_in, p_out, relay, p_in, q_out, q_in, z_out, z_in, p_sem, q_sem, z_sem = scratch
    c, p, q, z = here
    up, down = device(c, (p + 1) % NP, q, z), device(c, (p + 3) % NP, q, z)
    copies = list(core.values())

    def fill(slot, k, h, relayed):
        pp = (p + k) % NP

        def body(i, carry):
            value = part[c, pp, 2 * h + i] + core_in[pp, 2 * h + i]
            if relayed:
                value = value + relay[h, i].astype(F32)
            p_out[slot, i] = value.astype(BF16)
            return carry

        lax.fori_loop(0, 2, body, 0)

    core[2].wait_recv()
    fill(0, 2, 0, False)
    far = [send(p_out.at[0], relay.at[0], p_sem, 0, up)]
    fill(1, 2, 1, False)
    far.append(send(p_out.at[1], relay.at[1], p_sem, 1, down))
    core[1].wait_recv()
    fill(2, 1, 1, False)
    near = [send(p_out.at[2], p_in.at[0, 1], p_sem, 2, up)]
    core[3].wait_recv()
    fill(3, 3, 0, False)
    near.append(send(p_out.at[3], p_in.at[1, 0], p_sem, 3, down))
    far[0].wait_recv()
    fill(4, 1, 0, True)
    near.append(send(p_out.at[4], p_in.at[0, 0], p_sem, 4, up))
    far[1].wait_recv()
    fill(5, 3, 1, True)
    near.append(send(p_out.at[5], p_in.at[1, 1], p_sem, 5, down))
    copies += far + near
    core[0].wait_recv()
    for copy in near:
        copy.wait_recv()

    def chunk(qq):
        h, i = qq // 2, qq % 2
        total = part[c, p, qq] + core_in[p, qq]
        return total + p_in[0, h, i].astype(F32) + p_in[1, h, i].astype(F32)

    ring = {}
    dots = own
    for k in (2, 1, 3):
        qq = (q + k) % NQ
        value = chunk(qq)
        q_out[k - 1] = value.astype(BF16)
        if total is not None:
            dots = dots + eighths(weigh(qq) * value)
        ring[k] = send(q_out.at[k - 1], q_in.at[k - 1], q_sem, k, device(c, p, qq, z))
        copies.append(ring[k])
    value = chunk(q)
    if total is not None:
        total.start("q", dots + eighths(weigh(q) * value))
    for k in (1, 3, 2):
        ring[k].wait_recv()
        value = value + q_in[k - 1].astype(F32)
    z_out[...] = value.astype(BF16)
    ring = {}
    order = (4, 3, 5, 2, 6, 1, 7)
    for k in order:
        zz = (z + k) % NZ
        ring[k] = send(z_out.at[zz], z_in.at[k - 1], z_sem, k, device(c, p, q, zz))
        copies.append(ring[k])
    if total is not None:
        total.start("z", total.finish())
    rows = z_out[z].astype(F32)
    for k in order[::-1]:
        ring[k].wait_recv()
        rows = rows + z_in[k - 1].astype(F32)
    if total is not None:
        total.start("rest", total.finish())
    for copy in copies:
        copy.wait_send()
    return rows


class Sum:
    def __init__(self, here, refs):
        self.here = here
        self.slots, self.sems = refs
        self.copies = []

    def start(self, stage, tile):
        c, p, q, z = self.here
        slots, sems = self.slots, self.sems
        at, others = {
            "z": (z, [device(c, p, q, (z + k) % NZ) for k in range(1, NZ)]),
            "q": (8 + q, [device(c, p, (q + k) % NQ, z) for k in range(1, NQ)]),
            "rest": (12 + p, [device(c, (p + k) % NP, q, z) for k in range(1, NP)]),
        }[stage]
        first = {"z": 0, "q": 8, "rest": 12}[stage]
        self.used = (first, first + (8 if stage != "q" else 4))
        mine = slots.at[at]
        mine[...] = tile
        self.now = [send(mine, mine, sems, first + k, d) for k, d in enumerate(others)]
        if stage == "rest":
            across = slots.at[16 + p]
            self.now += [send(mine, across, sems, 16 + k, device(1 - c, q, (p + k) % NQ, z)) for k in range(NQ)]
        self.copies += self.now

    def finish(self):
        for copy in self.now:
            copy.wait_recv()
        begin, end = self.used
        total = self.slots[begin]
        for k in range(begin + 1, min(end, begin + 4)):
            total = total + self.slots[k]
        if end > begin + 4:
            rest = self.slots[begin + 4]
            for k in range(begin + 5, end):
                rest = rest + self.slots[k]
            total = total + rest
        return total

    def close(self):
        tile = self.finish()
        for copy in self.copies:
            copy.wait_send()
        return all_of(tile)


def gather(here, rows, out, sems, total=None, tile=None, scales=None, scale_sems=None, meanwhile=None):
    c, p, q, z = here
    c_sem, p_sem, q_sem, z_sem = sems
    other = device(1 - c, q, p, z)
    copies, core = [], []

    def pause(i):
        if meanwhile is not None:
            meanwhile(i)

    def across(ref):
        core.append(send(ref, ref, c_sem, len(core), other))

    out[c, p, q, z] = rows.astype(BF16)
    mine = out.at[c, p, q, z]
    order = (4, 3, 5, 2, 6, 1, 7)
    ring = [send(mine, mine, z_sem, k, device(c, p, q, (z + k) % NZ)) for k in order]
    if scales is not None:
        mine = scales.at[q, z]
        ring += [send(mine, mine, scale_sems, k, device(c, p, q, (z + k) % NZ)) for k in order]
    if total is not None:
        total.start("z", tile)
    pause(0)
    for copy in ring:
        copy.wait_recv()
    copies += ring

    pieces = {}

    def along(j, qq):
        ref = out.at[c, p, qq]
        for k in (2, 1, 3):
            pieces[j, k] = send(ref, ref, p_sem, 4 * j + k, device(c, (p + k) % NP, q, z))
        across(ref)

    mine = out.at[c, p, q]
    ring = {k: send(mine, mine, q_sem, k, device(c, p, (q + k) % NQ, z)) for k in (2, 1, 3)}
    copies += ring.values()
    if scales is not None:
        mine = scales.at[q]
        beside = [send(mine, mine, scale_sems, 8 + k, device(c, p, (q + k) % NQ, z)) for k in (2, 1, 3)]
        copies += beside
    along(0, q)
    if total is not None:
        total.start("q", total.finish())
    pause(1)
    steps = (0, 1, 3, 2)
    for j in range(1, NQ):
        ring[steps[j]].wait_recv()
        along(j, (q - steps[j] + NQ) % NQ)
    if total is not None:
        total.start("rest", total.finish())
    pause(2)
    if scales is not None:
        for copy in beside:
            copy.wait_recv()
    for j in range(NQ):
        for k in (1, 3, 2):
            pieces[j, k].wait_recv()
            across(out.at[c, (p - k + NP) % NP, (q - steps[j] + NQ) % NQ])
    for copy in core:
        copy.wait_recv()
    for copy in copies + core + list(pieces.values()):
        copy.wait_send()


def folded(values):
    tile = values[0:8]
    for k in range(1, ROWS // 8):
        tile = tile + values[8 * k : 8 * k + 8]
    return tile


def eighths(values):
    tile = folded(values[0])
    for k in range(1, NZ):
        tile = tile + folded(values[k])
    return tile


def all_of(tile):
    return jnp.sum(tile, keepdims=True)


def masks(runs, counts, mask, begin, end):
    columns = lax.broadcasted_iota(jnp.int32, (TILE, TILE), 1)

    def group(g, carry):
        both = jnp.concatenate([runs[g, s] for s in range(SLOTS)], axis=0).T
        live = counts[g]
        for s in range(SLOTS):
            length = jnp.where(s < live, both[:, 2 * s + 1 : 2 * s + 2], 0)
            seen = ((columns - both[:, 2 * s : 2 * s + 1]) & (TILE - 1)) < length
            mask[g, s] = jnp.where(seen, 1.0, 0.0).astype(BF16)
        return carry

    lax.fori_loop(begin, end, group, 0)


def widen(narrow, wide):
    def body(i, carry):
        at = pl.multiple_of(i * TILE, TILE)
        wide[pl.ds(at, TILE)] = narrow[pl.ds(at, TILE)].astype(F32)
        return carry

    lax.fori_loop(0, SUBS // TILE, body, 0)


def columns_of(scales, wide):
    rows = lax.broadcasted_iota(jnp.int32, (ROWS, R), 0)
    lanes = lax.broadcasted_iota(jnp.int32, (ROWS, R), 1)

    def body(i, carry):
        for z in range(NZ):
            picked = jnp.where(rows == lanes, scales[i, z, 0:1], 0.0)
            wide[i, z] = jnp.broadcast_to(jnp.sum(picked, axis=1, keepdims=True), (ROWS, R))
        return carry

    lax.fori_loop(0, NQ, body, 0)


def block_sums(core, whole, words, subs, tables, mask, ratings, part):
    user_tile, word_tile, subreddit = tables

    def group(n, carry):
        g = 2 * n + core
        xl, z = n % 2, n // 2

        def rows_at(ref, u, y):
            x = 2 * u + xl
            return ref.at[core, x * (1 - core) + y * core, y * (1 - core) + x * core, z]

        work = []
        for s in range(SLOTS):
            u = user_tile[s, g]
            rows = jnp.concatenate([rows_at(whole, u, y)[...] for y in range(4)], axis=0)
            products = words[word_tile[s, g]] * subs[pl.ds(subreddit[s, g], 1)].astype(BF16)
            scores = lax.dot_general(rows, products, (((1,), (1,)), ((), ())), preferred_element_type=F32)
            work.append((s, u, products, scores))
        top, low = [], []
        for s, u, products, scores in work:
            if ratings is not None:
                scores = ratings[g, s].astype(F32) - scores
            weights = scores.astype(BF16) * mask[g, s]
            lower = weights * jnp.full((TILE, TILE), u, jnp.int32).astype(F32).astype(BF16)
            top.append(weights - lower)
            low.append(lower)
        both = jnp.concatenate([jnp.concatenate(top, 1), jnp.concatenate(low, 1)], 0)
        products = jnp.concatenate([w[2] for w in work], 0)
        sums = jnp.dot(both, products, preferred_element_type=F32)
        for u in range(UT):
            for y in range(4):
                at = u * TILE + ROWS * y
                rows_at(part, u, y)[...] = sums[at : at + ROWS]
        return carry

    lax.fori_loop(0, GROUPS // 2, group, 0)


DMA = pltpu.SemaphoreType.DMA
SCATTER_SCRATCH = [
    pltpu.VMEM((NP, NQ, NZ, ROWS, R), F32),
    pltpu.VMEM((6, 2, NZ, ROWS, R), BF16),
    pltpu.VMEM((2, 2, NZ, ROWS, R), BF16),
    pltpu.VMEM((2, 2, 2, NZ, ROWS, R), BF16),
    pltpu.VMEM((NQ - 1, NZ, ROWS, R), BF16),
    pltpu.VMEM((NQ - 1, NZ, ROWS, R), BF16),
    pltpu.VMEM((NZ, ROWS, R), BF16),
    pltpu.VMEM((NZ - 1, ROWS, R), BF16),
    DMA((2, 6)),
    DMA((2, NQ)),
    DMA((2, NZ)),
]
GATHER_SCRATCH = [DMA((2, NP * NQ)), DMA((2, NP * NQ)), DMA((2, NQ)), DMA((2, NZ))]
SUM_SCRATCH = [pltpu.VMEM((20, 8, R), F32), DMA((2, 20))]
WHOLE = pltpu.VMEM((2, NP, NQ, NZ, ROWS, R), BF16)
BLOCKS = pltpu.VMEM((GROUPS, SLOTS, TILE, TILE), BF16)
SCRATCH = [WHOLE] * 3 + [
    pltpu.VMEM((2, NP, NQ, NZ, ROWS, R), F32),
    BLOCKS,
    BLOCKS,
    DMA,
    DMA((2, NP)),
    pltpu.VMEM((SUBS, R), F32),
    pltpu.VMEM((NQ, NZ, 8, R), F32),
    pltpu.VMEM((NQ, NZ, ROWS, R), F32),
    DMA((2, 12)),
]
N_S, N_G, N_SUM, N_OWN = len(SCATTER_SCRATCH), len(GATHER_SCRATCH), len(SUM_SCRATCH), len(SCRATCH)


def step_kernel(start, activity, words, subs, runs, counts, user_tile, word_tile, subreddit, ratings, out, left, *scratch):
    whole0, whole1, whole2, part, mask, held, fetch_sem, core_sem, wide, scales, scale, scale_sems = scratch[:N_OWN]
    scatter = scratch[N_OWN : N_OWN + N_S]
    at = N_OWN + N_S
    gather_sems = scratch[at : at + N_G]
    sums = [scratch[at + N_G + i * N_SUM : at + N_G + (i + 1) * N_SUM] for i in range(4)]
    tables = (user_tile, word_tile, subreddit)
    here = place()
    c, p, q, z = here
    fetch = pltpu.make_async_copy(ratings, held, fetch_sem)
    fetch.start()
    padded = jnp.concatenate([activity[...], jnp.zeros((1, R - ROWS), F32)], axis=1)
    scales[q, z] = jnp.broadcast_to(padded, (8, R))
    enter(here)

    def blocks(whole, values):
        block_sums(1 - c, whole, words, wide, tables, mask, values, part)
        core = to_partner(here, part, scatter[0], core_sem)
        block_sums(c, whole, words, wide, tables, mask, values, part)
        return core

    cuts = (0, 11, 22, GROUPS)

    def meanwhile(i):
        if i == 0:
            widen(subs, wide)
        masks(runs, counts, mask, cuts[i], cuts[i + 1])

    gather(here, start[...], whole0, gather_sems, scales=scales, scale_sems=scale_sems, meanwhile=meanwhile)
    columns_of(scales, scale)
    fetch.wait()
    core = blocks(whole0, held)
    scaled = scale[q, z]
    r = scaled * reduce_scatter(here, part, core, scatter) - RIDGE * start[...]
    norm = Sum(here, sums[0])
    gather(here, r, whole1, gather_sems, norm, folded(r * r))

    core = blocks(whole1, None)
    rr = norm.close()
    along = Sum(here, sums[1])
    rows = reduce_scatter(
        here, part, core, scatter, along, lambda qq: scale[qq] * whole1[c, p, qq].astype(F32), RIDGE * folded(r * r)
    )
    image = scaled * rows + RIDGE * r
    step = rr / along.close()
    solution = start[...] + step * r
    later = r - step * image
    norm = Sum(here, sums[2])
    gather(here, later, whole2, gather_sems, norm, folded(later * later))

    core = blocks(whole2, None)
    new = norm.close()
    ratio = new / rr
    d = later + ratio * r

    def weigh(qq):
        return scale[qq] * (whole2[c, p, qq].astype(F32) + ratio[:, :, None] * whole1[c, p, qq].astype(F32))

    along = Sum(here, sums[3])
    rest = RIDGE * later + ratio * image
    rows = reduce_scatter(here, part, core, scatter, along, weigh, folded(d * rest))
    step = new / along.close()
    out[...] = solution + step * d
    left[...] = later - step * (scaled * rows + rest)


def on_device(
    factor_start,
    activity,
    word_factors,
    sub_factors,
    ratings,
    user_tile,
    word_tile,
    subreddit,
    counts,
    runs,
):
    table = pl.BlockSpec(memory_space=pltpu.SMEM)
    block = jax.ShapeDtypeStruct((ROWS, R), F32)
    return tuple(
        pl.pallas_call(
            step_kernel,
            out_shape=[block, block],
            in_specs=[VMEM] * 5 + [table] * 4 + [pl.BlockSpec(memory_space=pl.ANY)],
            out_specs=[VMEM] * 2,
            scratch_shapes=SCRATCH + SCATTER_SCRATCH + GATHER_SCRATCH + SUM_SCRATCH * 4,
            compiler_params=pltpu.CompilerParams(
                collective_id=0, has_side_effects=True, vmem_limit_bytes=50 << 20
            ),
            name="step",
        )(
            factor_start,
            activity.reshape(1, ROWS),
            word_factors[0],
            sub_factors,
            runs[0, 0],
            counts[0, 0],
            user_tile[0, 0].T,
            word_tile[0, 0].T,
            subreddit[0, 0].T,
            ratings[0, 0],
        )
    )


def solution(mesh):
    placed = (
        P(("loop", "own"), None),
        P(("loop", "own")),
        P("loop", None, None, None),
        P(),
        P("loop", "own", None, None, None, None),
        P("loop", "own", None, None),
        P("loop", "own", None, None),
        P("loop", "own", None, None),
        P("loop", "own", None),
        P("loop", "own", None, None, None, None),
    )
    return jax.shard_map(
        on_device,
        mesh=mesh,
        in_specs=placed,
        out_specs=(P(("loop", "own"), None), P(("loop", "own"), None)),
        check_vma=False,
    )
```

```python
import jax
import jax.numpy as jnp
from jax import lax
from jax.experimental import pallas as pl
from jax.experimental.pallas import tpu as pltpu
from jax.sharding import PartitionSpec as P

TILE = 128
R = 128
UT = 2
SLOTS = 8
SUBS = 2048
GROUPS = 32
NP = 4
NQ = 4
NZ = 8
ROWS = 32
RIDGE = 0.05
MESH = pl.DeviceIdType.MESH
F32 = jnp.float32
BF16 = jnp.bfloat16
VMEM = pl.BlockSpec(memory_space=pltpu.VMEM)


def place():
    loop = lax.axis_index("loop")
    own = lax.axis_index("own")
    c = loop % 2
    x = (own // 4) * 2 + (loop // 2) % 2
    y = own % 4
    z = loop // 4
    return c, x * (1 - c) + y * c, y * (1 - c) + x * c, z


def device(c, p, q, z):
    x = p * (1 - c) + q * c
    y = q * (1 - c) + p * c
    return {"loop": (z * 2 + x % 2) * 2 + c, "own": (x // 2) * 4 + y}


def send(src, dst, sems, k, to):
    copy = pltpu.make_async_remote_copy(
        src_ref=src,
        dst_ref=dst,
        send_sem=sems.at[0, k],
        recv_sem=sems.at[1, k],
        device_id=to,
        device_id_type=MESH,
    )
    copy.start()
    return copy


def enter(here):
    c, p, q, z = here
    barrier = pltpu.get_barrier_semaphore()
    partners = [device(1 - c, q, (p + k) % NQ, z) for k in range(NQ)]
    partners += [device(1 - c, (q + k) % NP, p, z) for k in range(1, NP)]
    partners += [device(c, (p + k) % NP, q, z) for k in range(1, NP)]
    partners += [device(c, p, (q + k) % NQ, z) for k in range(1, NQ)]
    partners += [device(c, p, q, (z + k) % NZ) for k in range(1, NZ)]
    for partner in partners:
        pl.semaphore_signal(barrier, inc=1, device_id=partner, device_id_type=MESH)
    pl.semaphore_wait(barrier, len(partners))


def to_partner(here, part, core_in, c_sem):
    c, p, q, z = here
    core = {}
    for k in (2, 1, 3, 0):
        pp = (q + k) % NP
        core[k] = send(part.at[1 - c, pp], core_in.at[pp], c_sem, k, device(1 - c, q, p, z))
    return core


def reduce_scatter(here, part, core, scratch, total=None, weigh=None, own=None):
    core_in, p_out, relay, p_in, q_out, q_in, z_out, z_in, p_sem, q_sem, z_sem = scratch
    c, p, q, z = here
    up, down = device(c, (p + 1) % NP, q, z), device(c, (p + 3) % NP, q, z)
    copies = list(core.values())

    def fill(slot, k, h, relayed):
        pp = (p + k) % NP

        def body(i, carry):
            value = part[c, pp, 2 * h + i] + core_in[pp, 2 * h + i]
            if relayed:
                value = value + relay[h, i].astype(F32)
            p_out[slot, i] = value.astype(BF16)
            return carry

        lax.fori_loop(0, 2, body, 0)

    core[2].wait_recv()
    fill(0, 2, 0, False)
    far = [send(p_out.at[0], relay.at[0], p_sem, 0, up)]
    fill(1, 2, 1, False)
    far.append(send(p_out.at[1], relay.at[1], p_sem, 1, down))
    core[1].wait_recv()
    fill(2, 1, 1, False)
    near = [send(p_out.at[2], p_in.at[0, 1], p_sem, 2, up)]
    core[3].wait_recv()
    fill(3, 3, 0, False)
    near.append(send(p_out.at[3], p_in.at[1, 0], p_sem, 3, down))
    far[0].wait_recv()
    fill(4, 1, 0, True)
    near.append(send(p_out.at[4], p_in.at[0, 0], p_sem, 4, up))
    far[1].wait_recv()
    fill(5, 3, 1, True)
    near.append(send(p_out.at[5], p_in.at[1, 1], p_sem, 5, down))
    copies += far + near
    core[0].wait_recv()
    for copy in near:
        copy.wait_recv()

    def chunk(qq):
        h, i = qq // 2, qq % 2
        total = part[c, p, qq] + core_in[p, qq]
        return total + p_in[0, h, i].astype(F32) + p_in[1, h, i].astype(F32)

    ring = {}
    dots = own
    for k in (2, 1, 3):
        qq = (q + k) % NQ
        value = chunk(qq)
        q_out[k - 1] = value.astype(BF16)
        if total is not None:
            dots = dots + eighths(weigh(qq) * value)
        ring[k] = send(q_out.at[k - 1], q_in.at[k - 1], q_sem, k, device(c, p, qq, z))
        copies.append(ring[k])
    value = chunk(q)
    if total is not None:
        total.start("q", dots + eighths(weigh(q) * value))
    for k in (1, 3, 2):
        ring[k].wait_recv()
        value = value + q_in[k - 1].astype(F32)
    z_out[...] = value.astype(BF16)
    ring = {}
    order = (4, 3, 5, 2, 6, 1, 7)
    for k in order:
        zz = (z + k) % NZ
        ring[k] = send(z_out.at[zz], z_in.at[k - 1], z_sem, k, device(c, p, q, zz))
        copies.append(ring[k])
    if total is not None:
        total.start("z", total.finish())
    rows = z_out[z].astype(F32)
    for k in order[::-1]:
        ring[k].wait_recv()
        rows = rows + z_in[k - 1].astype(F32)
    if total is not None:
        total.start("rest", total.finish())
    for copy in copies:
        copy.wait_send()
    return rows


class Sum:
    def __init__(self, here, refs):
        self.here = here
        self.slots, self.sems = refs
        self.copies = []

    def start(self, stage, tile):
        c, p, q, z = self.here
        slots, sems = self.slots, self.sems
        at, others = {
            "z": (z, [device(c, p, q, (z + k) % NZ) for k in range(1, NZ)]),
            "q": (8 + q, [device(c, p, (q + k) % NQ, z) for k in range(1, NQ)]),
            "rest": (12 + p, [device(c, (p + k) % NP, q, z) for k in range(1, NP)]),
        }[stage]
        first = {"z": 0, "q": 8, "rest": 12}[stage]
        self.used = (first, first + (8 if stage != "q" else 4))
        mine = slots.at[at]
        mine[...] = tile
        self.now = [send(mine, mine, sems, first + k, d) for k, d in enumerate(others)]
        if stage == "rest":
            across = slots.at[16 + p]
            self.now += [send(mine, across, sems, 16 + k, device(1 - c, q, (p + k) % NQ, z)) for k in range(NQ)]
        self.copies += self.now

    def finish(self):
        for copy in self.now:
            copy.wait_recv()
        begin, end = self.used
        total = self.slots[begin]
        for k in range(begin + 1, min(end, begin + 4)):
            total = total + self.slots[k]
        if end > begin + 4:
            rest = self.slots[begin + 4]
            for k in range(begin + 5, end):
                rest = rest + self.slots[k]
            total = total + rest
        return total

    def close(self):
        tile = self.finish()
        for copy in self.copies:
            copy.wait_send()
        return all_of(tile)


def gather(here, rows, out, sems, total=None, tile=None, scales=None, scale_sems=None, meanwhile=None):
    c, p, q, z = here
    c_sem, p_sem, q_sem, z_sem = sems
    other = device(1 - c, q, p, z)
    copies, core = [], []

    def pause(i):
        if meanwhile is not None:
            meanwhile(i)

    def across(ref):
        core.append(send(ref, ref, c_sem, len(core), other))

    out[c, p, q, z] = rows.astype(BF16)
    mine = out.at[c, p, q, z]
    order = (4, 3, 5, 2, 6, 1, 7)
    ring = [send(mine, mine, z_sem, k, device(c, p, q, (z + k) % NZ)) for k in order]
    if scales is not None:
        mine = scales.at[q, z]
        ring += [send(mine, mine, scale_sems, k, device(c, p, q, (z + k) % NZ)) for k in order]
    if total is not None:
        total.start("z", tile)
    pause(0)
    for copy in ring:
        copy.wait_recv()
    copies += ring

    pieces = {}

    def along(j, qq):
        ref = out.at[c, p, qq]
        for k in (2, 1, 3):
            pieces[j, k] = send(ref, ref, p_sem, 4 * j + k, device(c, (p + k) % NP, q, z))
        across(ref)

    mine = out.at[c, p, q]
    ring = {k: send(mine, mine, q_sem, k, device(c, p, (q + k) % NQ, z)) for k in (2, 1, 3)}
    copies += ring.values()
    if scales is not None:
        mine = scales.at[q]
        beside = [send(mine, mine, scale_sems, 8 + k, device(c, p, (q + k) % NQ, z)) for k in (2, 1, 3)]
        copies += beside
    along(0, q)
    if total is not None:
        total.start("q", total.finish())
    pause(1)
    steps = (0, 1, 3, 2)
    for j in range(1, NQ):
        ring[steps[j]].wait_recv()
        along(j, (q - steps[j] + NQ) % NQ)
    if total is not None:
        total.start("rest", total.finish())
    pause(2)
    if scales is not None:
        for copy in beside:
            copy.wait_recv()
    for j in range(NQ):
        for k in (1, 3, 2):
            pieces[j, k].wait_recv()
            across(out.at[c, (p - k + NP) % NP, (q - steps[j] + NQ) % NQ])
    for copy in core:
        copy.wait_recv()
    for copy in copies + core + list(pieces.values()):
        copy.wait_send()


def folded(values):
    tile = values[0:8]
    for k in range(1, ROWS // 8):
        tile = tile + values[8 * k : 8 * k + 8]
    return tile


def eighths(values):
    tile = folded(values[0])
    for k in range(1, NZ):
        tile = tile + folded(values[k])
    return tile


def all_of(tile):
    return jnp.sum(tile, keepdims=True)


def masks(runs, counts, mask, begin, end):
    columns = lax.broadcasted_iota(jnp.int32, (TILE, TILE), 1)

    def group(g, carry):
        both = jnp.concatenate([runs[g, s] for s in range(SLOTS)], axis=0).T
        live = counts[g]
        for s in range(SLOTS):
            length = jnp.where(s < live, both[:, 2 * s + 1 : 2 * s + 2], 0)
            seen = ((columns - both[:, 2 * s : 2 * s + 1]) & (TILE - 1)) < length
            mask[g, s] = jnp.where(seen, 1.0, 0.0).astype(BF16)
        return carry

    lax.fori_loop(begin, end, group, 0)


def widen(narrow, wide):
    def body(i, carry):
        at = pl.multiple_of(i * TILE, TILE)
        wide[pl.ds(at, TILE)] = narrow[pl.ds(at, TILE)].astype(F32)
        return carry

    lax.fori_loop(0, SUBS // TILE, body, 0)


def columns_of(scales, wide):
    rows = lax.broadcasted_iota(jnp.int32, (ROWS, R), 0)
    lanes = lax.broadcasted_iota(jnp.int32, (ROWS, R), 1)

    def body(i, carry):
        for z in range(NZ):
            picked = jnp.where(rows == lanes, scales[i, z, 0:1], 0.0)
            wide[i, z] = jnp.broadcast_to(jnp.sum(picked, axis=1, keepdims=True), (ROWS, R))
        return carry

    lax.fori_loop(0, NQ, body, 0)


def block_sums(core, whole, words, subs, tables, mask, ratings, part):
    user_tile, word_tile, subreddit = tables

    def group(n, carry):
        g = 2 * n + core
        xl, z = n % 2, n // 2

        def rows_at(ref, u, y):
            x = 2 * u + xl
            return ref.at[core, x * (1 - core) + y * core, y * (1 - core) + x * core, z]

        zero = jnp.zeros((TILE, R), BF16)
        work = []
        for s in range(0, SLOTS, 2):
            pair = []
            for t in (s, s + 1):
                u = user_tile[t, g]
                rows = jnp.concatenate([rows_at(whole, u, y)[...] for y in range(4)], axis=0)
                products = words[word_tile[t, g]] * subs[pl.ds(subreddit[t, g], 1)].astype(BF16)
                pair.append((u, rows, products))
            (u0, v0, p0), (u1, v1, p1) = pair
            both = jnp.concatenate([jnp.concatenate([p0, zero], 1), jnp.concatenate([zero, p1], 1)], 0)
            scores = lax.dot_general(
                jnp.concatenate([v0, v1], 1), both, (((1,), (1,)), ((), ())), preferred_element_type=F32
            )
            work += [(s, u0, p0, scores[:, :TILE]), (s + 1, u1, p1, scores[:, TILE:])]
        top, low = [], []
        for s, u, products, scores in work:
            if ratings is not None:
                scores = ratings[g, s].astype(F32) - scores
            weights = scores.astype(BF16) * mask[g, s]
            lower = weights * jnp.full((TILE, TILE), u, jnp.int32).astype(F32).astype(BF16)
            top.append(weights - lower)
            low.append(lower)
        both = jnp.concatenate([jnp.concatenate(top, 1), jnp.concatenate(low, 1)], 0)
        products = jnp.concatenate([w[2] for w in work], 0)
        sums = jnp.dot(both, products, preferred_element_type=F32)
        for u in range(UT):
            for y in range(4):
                at = u * TILE + ROWS * y
                rows_at(part, u, y)[...] = sums[at : at + ROWS]
        return carry

    lax.fori_loop(0, GROUPS // 2, group, 0, unroll=4)


DMA = pltpu.SemaphoreType.DMA
SCATTER_SCRATCH = [
    pltpu.VMEM((NP, NQ, NZ, ROWS, R), F32),
    pltpu.VMEM((6, 2, NZ, ROWS, R), BF16),
    pltpu.VMEM((2, 2, NZ, ROWS, R), BF16),
    pltpu.VMEM((2, 2, 2, NZ, ROWS, R), BF16),
    pltpu.VMEM((NQ - 1, NZ, ROWS, R), BF16),
    pltpu.VMEM((NQ - 1, NZ, ROWS, R), BF16),
    pltpu.VMEM((NZ, ROWS, R), BF16),
    pltpu.VMEM((NZ - 1, ROWS, R), BF16),
    DMA((2, 6)),
    DMA((2, NQ)),
    DMA((2, NZ)),
]
GATHER_SCRATCH = [DMA((2, NP * NQ)), DMA((2, NP * NQ)), DMA((2, NQ)), DMA((2, NZ))]
SUM_SCRATCH = [pltpu.VMEM((20, 8, R), F32), DMA((2, 20))]
WHOLE = pltpu.VMEM((2, NP, NQ, NZ, ROWS, R), BF16)
BLOCKS = pltpu.VMEM((GROUPS, SLOTS, TILE, TILE), BF16)
INPUTS = [
    pltpu.VMEM((ROWS, R), F32),
    pltpu.VMEM((1, ROWS), F32),
    pltpu.VMEM((8, TILE, R), BF16),
    pltpu.VMEM((SUBS, R), BF16),
    pltpu.VMEM((GROUPS, SLOTS, 2, TILE), jnp.int32),
    pltpu.SMEM((GROUPS,), jnp.int32),
    pltpu.SMEM((SLOTS, GROUPS), jnp.int32),
    pltpu.SMEM((SLOTS, GROUPS), jnp.int32),
    pltpu.SMEM((SLOTS, GROUPS), jnp.int32),
    BLOCKS,
    DMA((10,)),
]
SCRATCH = [WHOLE] * 3 + [
    pltpu.VMEM((2, NP, NQ, NZ, ROWS, R), F32),
    BLOCKS,
    DMA((2, NP)),
    pltpu.VMEM((SUBS, R), F32),
    pltpu.VMEM((NQ, NZ, 8, R), F32),
    pltpu.VMEM((NQ, NZ, ROWS, R), F32),
    DMA((2, 12)),
]
N_S, N_G, N_SUM, N_OWN = len(SCATTER_SCRATCH), len(GATHER_SCRATCH), len(SUM_SCRATCH), len(SCRATCH)


def step_kernel(*refs):
    given, (out, left), scratch = refs[:10], refs[10:12], refs[12:]
    inputs, scratch = scratch[:11], scratch[11:]
    fetch_sems = inputs[-1]
    start, activity, words, subs, runs, counts, user_tile, word_tile, subreddit, held = inputs[:10]
    whole0, whole1, whole2, part, mask, core_sem, wide, scales, scale, scale_sems = scratch[:N_OWN]
    scatter = scratch[N_OWN : N_OWN + N_S]
    at = N_OWN + N_S
    gather_sems = scratch[at : at + N_G]
    sums = [scratch[at + N_G + i * N_SUM : at + N_G + (i + 1) * N_SUM] for i in range(4)]
    tables = (user_tile, word_tile, subreddit)
    here = place()
    c, p, q, z = here
    fetches = [pltpu.make_async_copy(given[i], inputs[i], fetch_sems.at[i]) for i in range(10)]
    for fetch in fetches:
        fetch.start()
    for fetch in fetches[:2]:
        fetch.wait()
    padded = jnp.concatenate([activity[...], jnp.zeros((1, R - ROWS), F32)], axis=1)
    scales[q, z] = jnp.broadcast_to(padded, (8, R))
    enter(here)
    for fetch in fetches[2:9]:
        fetch.wait()

    def blocks(whole, values):
        block_sums(1 - c, whole, words, wide, tables, mask, values, part)
        core = to_partner(here, part, scatter[0], core_sem)
        block_sums(c, whole, words, wide, tables, mask, values, part)
        return core

    cuts = (0, 11, 22, GROUPS)

    def meanwhile(i):
        if i == 0:
            widen(subs, wide)
        masks(runs, counts, mask, cuts[i], cuts[i + 1])

    gather(here, start[...], whole0, gather_sems, scales=scales, scale_sems=scale_sems, meanwhile=meanwhile)
    columns_of(scales, scale)
    fetches[9].wait()
    core = blocks(whole0, held)
    scaled = scale[q, z]
    r = scaled * reduce_scatter(here, part, core, scatter) - RIDGE * start[...]
    norm = Sum(here, sums[0])
    gather(here, r, whole1, gather_sems, norm, folded(r * r))

    core = blocks(whole1, None)
    rr = norm.close()
    along = Sum(here, sums[1])
    rows = reduce_scatter(
        here, part, core, scatter, along, lambda qq: scale[qq] * whole1[c, p, qq].astype(F32), RIDGE * folded(r * r)
    )
    image = scaled * rows + RIDGE * r
    step = rr / along.close()
    solution = start[...] + step * r
    later = r - step * image
    norm = Sum(here, sums[2])
    gather(here, later, whole2, gather_sems, norm, folded(later * later))

    core = blocks(whole2, None)
    new = norm.close()
    ratio = new / rr
    d = later + ratio * r

    def weigh(qq):
        return scale[qq] * (whole2[c, p, qq].astype(F32) + ratio[:, :, None] * whole1[c, p, qq].astype(F32))

    along = Sum(here, sums[3])
    rest = RIDGE * later + ratio * image
    rows = reduce_scatter(here, part, core, scatter, along, weigh, folded(d * rest))
    step = new / along.close()
    out[...] = solution + step * d
    left[...] = later - step * (scaled * rows + rest)


def on_device(
    factor_start,
    activity,
    word_factors,
    sub_factors,
    ratings,
    user_tile,
    word_tile,
    subreddit,
    counts,
    runs,
):
    block = jax.ShapeDtypeStruct((ROWS, R), F32)
    return tuple(
        pl.pallas_call(
            step_kernel,
            out_shape=[block, block],
            in_specs=[pl.BlockSpec(memory_space=pl.ANY)] * 10,
            out_specs=[VMEM] * 2,
            scratch_shapes=INPUTS + SCRATCH + SCATTER_SCRATCH + GATHER_SCRATCH + SUM_SCRATCH * 4,
            compiler_params=pltpu.CompilerParams(
                collective_id=0, has_side_effects=True, vmem_limit_bytes=60 * 1024 * 1024
            ),
            name="step",
        )(
            factor_start,
            activity.reshape(1, ROWS),
            word_factors[0],
            sub_factors,
            runs[0, 0],
            counts[0, 0],
            user_tile[0, 0].T,
            word_tile[0, 0].T,
            subreddit[0, 0].T,
            ratings[0, 0],
        )
    )


def solution(mesh):
    placed = (
        P(("loop", "own"), None),
        P(("loop", "own")),
        P("loop", None, None, None),
        P(),
        P("loop", "own", None, None, None, None),
        P("loop", "own", None, None),
        P("loop", "own", None, None),
        P("loop", "own", None, None),
        P("loop", "own", None),
        P("loop", "own", None, None, None, None),
    )
    return jax.shard_map(
        on_device,
        mesh=mesh,
        in_specs=placed,
        out_specs=(P(("loop", "own"), None), P(("loop", "own"), None)),
        check_vma=False,
    )
```

```python
import jax
import jax.numpy as jnp
from jax import lax
from jax.experimental import pallas as pl
from jax.experimental.pallas import tpu as pltpu
from jax.sharding import PartitionSpec as P

TILE = 128
R = 128
UT = 2
SLOTS = 8
SUBS = 2048
GROUPS = 32
NP = 4
NQ = 4
NZ = 8
HALF = NZ // 2
ROWS = 32
RIDGE = 0.05
MESH = pl.DeviceIdType.MESH
F32 = jnp.float32
BF16 = jnp.bfloat16
VMEM = pl.BlockSpec(memory_space=pltpu.VMEM)


def place():
    loop = lax.axis_index("loop")
    own = lax.axis_index("own")
    c = loop % 2
    x = (own // 4) * 2 + (loop // 2) % 2
    y = own % 4
    z = loop // 4
    return c, x * (1 - c) + y * c, y * (1 - c) + x * c, z


def device(c, p, q, z):
    x = p * (1 - c) + q * c
    y = q * (1 - c) + p * c
    return {"loop": (z * 2 + x % 2) * 2 + c, "own": (x // 2) * 4 + y}


def send(src, dst, sems, k, to):
    copy = pltpu.make_async_remote_copy(
        src_ref=src,
        dst_ref=dst,
        send_sem=sems.at[0, k],
        recv_sem=sems.at[1, k],
        device_id=to,
        device_id_type=MESH,
    )
    copy.start()
    return copy


def enter(here):
    c, p, q, z = here
    barrier = pltpu.get_barrier_semaphore()
    partners = [device(1 - c, q, (p + k) % NQ, z) for k in range(NQ)]
    partners += [device(1 - c, (q + k) % NP, p, z) for k in range(1, NP)]
    partners += [device(c, (p + k) % NP, q, z) for k in range(1, NP)]
    partners += [device(c, p, (q + k) % NQ, z) for k in range(1, NQ)]
    partners += [device(c, p, q, (z + k) % NZ) for k in range(1, NZ)]
    for partner in partners:
        pl.semaphore_signal(barrier, inc=1, device_id=partner, device_id_type=MESH)
    pl.semaphore_wait(barrier, len(partners))


def to_partner(here, part, core_in, c_sem, t):
    c, p, q, z = here
    zs = pl.ds(HALF * t, HALF)
    core = {}
    for k in (2, 1, 3, 0):
        pp = (q + k) % NP
        core[k] = send(part.at[1 - c, pp, :, zs], core_in.at[pp, :, zs], c_sem, NP * t + k, device(1 - c, q, p, z))
    return core


class FirstRing:
    def __init__(self, here, part, core, scratch, t):
        self.here, self.part, self.core, self.t = here, part, core, t
        self.core_in, self.p_out, self.relay, self.p_in = scratch[:4]
        self.sems = scratch[8]
        self.zs = pl.ds(HALF * t, HALF)

    def fill(self, slot, k, h, relayed):
        c, p, _, _ = self.here
        pp = (p + k) % NP
        zs = self.zs

        def body(i, carry):
            value = self.part[c, pp, 2 * h + i, zs] + self.core_in[pp, 2 * h + i, zs]
            if relayed:
                value = value + self.relay[h, i, zs].astype(F32)
            self.p_out[slot, i, zs] = value.astype(BF16)
            return carry

        lax.fori_loop(0, 2, body, 0)

    def go(self, slot, to, k):
        c, p, q, z = self.here
        source = self.p_out.at[slot, :, self.zs]
        return send(source, to.at[:, self.zs], self.sems, 6 * self.t + slot, device(c, (p + k) % NP, q, z))

    def start(self):
        self.core[2].wait_recv()
        self.fill(0, 2, 0, False)
        self.far = [self.go(0, self.relay.at[0], 1)]
        self.fill(1, 2, 1, False)
        self.far.append(self.go(1, self.relay.at[1], 3))
        self.core[1].wait_recv()
        self.fill(2, 1, 1, False)
        self.near = [self.go(2, self.p_in.at[0, 1], 1)]
        self.core[3].wait_recv()
        self.fill(3, 3, 0, False)
        self.near.append(self.go(3, self.p_in.at[1, 0], 3))

    def pass_on(self):
        self.far[0].wait_recv()
        self.fill(4, 1, 0, True)
        self.near.append(self.go(4, self.p_in.at[0, 0], 1))
        self.far[1].wait_recv()
        self.fill(5, 3, 1, True)
        self.near.append(self.go(5, self.p_in.at[1, 1], 3))

    def finish(self):
        self.core[0].wait_recv()
        for copy in self.near:
            copy.wait_recv()
        return list(self.core.values()) + self.far + self.near


def reduce_scatter(here, part, rings, scratch, total=None, weigh=None, own=None):
    core_in, p_out, relay, p_in, q_out, q_in, z_out, z_in, p_sem, q_sem, z_sem = scratch
    c, p, q, z = here
    copies = []
    for ring in rings:
        copies += ring.finish()

    def chunk(qq):
        h, i = qq // 2, qq % 2
        total = part[c, p, qq] + core_in[p, qq]
        return total + p_in[0, h, i].astype(F32) + p_in[1, h, i].astype(F32)

    ring = {}
    dots = own
    for k in (2, 1, 3):
        qq = (q + k) % NQ
        value = chunk(qq)
        q_out[k - 1] = value.astype(BF16)
        if total is not None:
            dots = dots + eighths(weigh(qq) * value)
        ring[k] = send(q_out.at[k - 1], q_in.at[k - 1], q_sem, k, device(c, p, qq, z))
        copies.append(ring[k])
    value = chunk(q)
    if total is not None:
        total.start("q", dots + eighths(weigh(q) * value))
    for k in (1, 3, 2):
        ring[k].wait_recv()
        value = value + q_in[k - 1].astype(F32)
    z_out[...] = value.astype(BF16)
    ring = {}
    order = (4, 3, 5, 2, 6, 1, 7)
    for k in order:
        zz = (z + k) % NZ
        ring[k] = send(z_out.at[zz], z_in.at[k - 1], z_sem, k, device(c, p, q, zz))
        copies.append(ring[k])
    if total is not None:
        total.start("z", total.finish())
    rows = z_out[z].astype(F32)
    for k in order[::-1]:
        ring[k].wait_recv()
        rows = rows + z_in[k - 1].astype(F32)
    if total is not None:
        total.start("rest", total.finish())
    for copy in copies:
        copy.wait_send()
    return rows


class Sum:
    def __init__(self, here, refs):
        self.here = here
        self.slots, self.sems = refs
        self.copies = []

    def start(self, stage, tile):
        c, p, q, z = self.here
        slots, sems = self.slots, self.sems
        at, others = {
            "z": (z, [device(c, p, q, (z + k) % NZ) for k in range(1, NZ)]),
            "q": (8 + q, [device(c, p, (q + k) % NQ, z) for k in range(1, NQ)]),
            "rest": (12 + p, [device(c, (p + k) % NP, q, z) for k in range(1, NP)]),
        }[stage]
        first = {"z": 0, "q": 8, "rest": 12}[stage]
        self.used = (first, first + (8 if stage != "q" else 4))
        mine = slots.at[at]
        mine[...] = tile
        self.now = [send(mine, mine, sems, first + k, d) for k, d in enumerate(others)]
        if stage == "rest":
            across = slots.at[16 + p]
            self.now += [send(mine, across, sems, 16 + k, device(1 - c, q, (p + k) % NQ, z)) for k in range(NQ)]
        self.copies += self.now

    def finish(self):
        for copy in self.now:
            copy.wait_recv()
        begin, end = self.used
        total = self.slots[begin]
        for k in range(begin + 1, min(end, begin + 4)):
            total = total + self.slots[k]
        if end > begin + 4:
            rest = self.slots[begin + 4]
            for k in range(begin + 5, end):
                rest = rest + self.slots[k]
            total = total + rest
        return total

    def close(self):
        tile = self.finish()
        for copy in self.copies:
            copy.wait_send()
        return all_of(tile)


def gather(here, rows, out, sems, total=None, tile=None, scales=None, scale_sems=None, meanwhile=None):
    c, p, q, z = here
    c_sem, p_sem, q_sem, z_sem = sems
    other = device(1 - c, q, p, z)
    copies, core = [], []

    def pause(i):
        if meanwhile is not None:
            meanwhile(i)

    def across(ref):
        core.append(send(ref, ref, c_sem, len(core), other))

    out[c, p, q, z] = rows.astype(BF16)
    mine = out.at[c, p, q, z]
    order = (4, 3, 5, 2, 6, 1, 7)
    ring = [send(mine, mine, z_sem, k, device(c, p, q, (z + k) % NZ)) for k in order]
    if scales is not None:
        mine = scales.at[q, z]
        ring += [send(mine, mine, scale_sems, k, device(c, p, q, (z + k) % NZ)) for k in order]
    if total is not None:
        total.start("z", tile)
    pause(0)
    for copy in ring:
        copy.wait_recv()
    copies += ring

    pieces = {}

    def along(j, qq):
        ref = out.at[c, p, qq]
        for k in (2, 1, 3):
            pieces[j, k] = send(ref, ref, p_sem, 4 * j + k, device(c, (p + k) % NP, q, z))
        across(ref)

    mine = out.at[c, p, q]
    ring = {k: send(mine, mine, q_sem, k, device(c, p, (q + k) % NQ, z)) for k in (2, 1, 3)}
    copies += ring.values()
    if scales is not None:
        mine = scales.at[q]
        beside = [send(mine, mine, scale_sems, 8 + k, device(c, p, (q + k) % NQ, z)) for k in (2, 1, 3)]
        copies += beside
    along(0, q)
    if total is not None:
        total.start("q", total.finish())
    pause(1)
    steps = (0, 1, 3, 2)
    for j in range(1, NQ):
        ring[steps[j]].wait_recv()
        along(j, (q - steps[j] + NQ) % NQ)
    if total is not None:
        total.start("rest", total.finish())
    pause(2)
    if scales is not None:
        for copy in beside:
            copy.wait_recv()
    for j in range(NQ):
        for k in (1, 3, 2):
            pieces[j, k].wait_recv()
            across(out.at[c, (p - k + NP) % NP, (q - steps[j] + NQ) % NQ])
    for copy in core:
        copy.wait_recv()
    for copy in copies + core + list(pieces.values()):
        copy.wait_send()


def folded(values):
    tile = values[0:8]
    for k in range(1, ROWS // 8):
        tile = tile + values[8 * k : 8 * k + 8]
    return tile


def eighths(values):
    tile = folded(values[0])
    for k in range(1, NZ):
        tile = tile + folded(values[k])
    return tile


def all_of(tile):
    return jnp.sum(tile, keepdims=True)


def masks(runs, counts, mask, begin, end):
    columns = lax.broadcasted_iota(jnp.int32, (TILE, TILE), 1)

    def group(g, carry):
        both = jnp.concatenate([runs[g, s] for s in range(SLOTS)], axis=0).T
        live = counts[g]
        for s in range(SLOTS):
            length = jnp.where(s < live, both[:, 2 * s + 1 : 2 * s + 2], 0)
            seen = ((columns - both[:, 2 * s : 2 * s + 1]) & (TILE - 1)) < length
            mask[g, s] = jnp.where(seen, 1.0, 0.0).astype(BF16)
        return carry

    lax.fori_loop(begin, end, group, 0)


def widen(narrow, wide):
    def body(i, carry):
        at = pl.multiple_of(i * TILE, TILE)
        wide[pl.ds(at, TILE)] = narrow[pl.ds(at, TILE)].astype(F32)
        return carry

    lax.fori_loop(0, SUBS // TILE, body, 0)


def columns_of(scales, wide):
    rows = lax.broadcasted_iota(jnp.int32, (ROWS, R), 0)
    lanes = lax.broadcasted_iota(jnp.int32, (ROWS, R), 1)

    def body(i, carry):
        for z in range(NZ):
            picked = jnp.where(rows == lanes, scales[i, z, 0:1], 0.0)
            wide[i, z] = jnp.broadcast_to(jnp.sum(picked, axis=1, keepdims=True), (ROWS, R))
        return carry

    lax.fori_loop(0, NQ, body, 0)


def block_sums(core_of, begin, end, whole, words, subs, tables, mask, ratings, part):
    user_tile, word_tile, subreddit = tables

    def group(n, carry):
        core = core_of(n)
        g = 2 * n + core
        xl, z = n % 2, n // 2

        def rows_at(ref, u, y):
            x = 2 * u + xl
            return ref.at[core, x * (1 - core) + y * core, y * (1 - core) + x * core, z]

        zero = jnp.zeros((TILE, R), BF16)
        work = []
        for s in range(0, SLOTS, 2):
            pair = []
            for t in (s, s + 1):
                u = user_tile[t, g]
                rows = jnp.concatenate([rows_at(whole, u, y)[...] for y in range(4)], axis=0)
                products = words[word_tile[t, g]] * subs[pl.ds(subreddit[t, g], 1)].astype(BF16)
                pair.append((u, rows, products))
            (u0, v0, p0), (u1, v1, p1) = pair
            both = jnp.concatenate([jnp.concatenate([p0, zero], 1), jnp.concatenate([zero, p1], 1)], 0)
            scores = lax.dot_general(
                jnp.concatenate([v0, v1], 1), both, (((1,), (1,)), ((), ())), preferred_element_type=F32
            )
            work += [(s, u0, p0, scores[:, :TILE]), (s + 1, u1, p1, scores[:, TILE:])]
        top, low = [], []
        for s, u, products, scores in work:
            if ratings is not None:
                scores = ratings[g, s].astype(F32) - scores
            weights = scores.astype(BF16) * mask[g, s]
            lower = weights * jnp.full((TILE, TILE), u, jnp.int32).astype(F32).astype(BF16)
            top.append(weights - lower)
            low.append(lower)
        both = jnp.concatenate([jnp.concatenate(top, 1), jnp.concatenate(low, 1)], 0)
        products = jnp.concatenate([w[2] for w in work], 0)
        sums = jnp.dot(both, products, preferred_element_type=F32)
        for u in range(UT):
            for y in range(4):
                at = u * TILE + ROWS * y
                rows_at(part, u, y)[...] = sums[at : at + ROWS]
        return carry

    lax.fori_loop(begin, end, group, 0, unroll=4)


DMA = pltpu.SemaphoreType.DMA
SCATTER_SCRATCH = [
    pltpu.VMEM((NP, NQ, NZ, ROWS, R), F32),
    pltpu.VMEM((6, 2, NZ, ROWS, R), BF16),
    pltpu.VMEM((2, 2, NZ, ROWS, R), BF16),
    pltpu.VMEM((2, 2, 2, NZ, ROWS, R), BF16),
    pltpu.VMEM((NQ - 1, NZ, ROWS, R), BF16),
    pltpu.VMEM((NQ - 1, NZ, ROWS, R), BF16),
    pltpu.VMEM((NZ, ROWS, R), BF16),
    pltpu.VMEM((NZ - 1, ROWS, R), BF16),
    DMA((2, 12)),
    DMA((2, NQ)),
    DMA((2, NZ)),
]
GATHER_SCRATCH = [DMA((2, NP * NQ)), DMA((2, NP * NQ)), DMA((2, NQ)), DMA((2, NZ))]
SUM_SCRATCH = [pltpu.VMEM((20, 8, R), F32), DMA((2, 20))]
WHOLE = pltpu.VMEM((2, NP, NQ, NZ, ROWS, R), BF16)
BLOCKS = pltpu.VMEM((GROUPS, SLOTS, TILE, TILE), BF16)
INPUTS = [
    pltpu.VMEM((ROWS, R), F32),
    pltpu.VMEM((1, ROWS), F32),
    pltpu.VMEM((8, TILE, R), BF16),
    pltpu.VMEM((SUBS, R), BF16),
    pltpu.VMEM((GROUPS, SLOTS, 2, TILE), jnp.int32),
    pltpu.SMEM((GROUPS,), jnp.int32),
    pltpu.SMEM((SLOTS, GROUPS), jnp.int32),
    pltpu.SMEM((SLOTS, GROUPS), jnp.int32),
    pltpu.SMEM((SLOTS, GROUPS), jnp.int32),
    BLOCKS,
    DMA((10,)),
]
SCRATCH = [WHOLE] * 3 + [
    pltpu.VMEM((2, NP, NQ, NZ, ROWS, R), F32),
    BLOCKS,
    DMA((2, 2 * NP)),
    pltpu.VMEM((SUBS, R), F32),
    pltpu.VMEM((NQ, NZ, 8, R), F32),
    pltpu.VMEM((NQ, NZ, ROWS, R), F32),
    DMA((2, 12)),
]
N_S, N_G, N_SUM, N_OWN = len(SCATTER_SCRATCH), len(GATHER_SCRATCH), len(SUM_SCRATCH), len(SCRATCH)


def step_kernel(*refs):
    given, (out, left), scratch = refs[:10], refs[10:12], refs[12:]
    inputs, scratch = scratch[:11], scratch[11:]
    fetch_sems = inputs[-1]
    start, activity, words, subs, runs, counts, user_tile, word_tile, subreddit, held = inputs[:10]
    whole0, whole1, whole2, part, mask, core_sem, wide, scales, scale, scale_sems = scratch[:N_OWN]
    scatter = scratch[N_OWN : N_OWN + N_S]
    at = N_OWN + N_S
    gather_sems = scratch[at : at + N_G]
    sums = [scratch[at + N_G + i * N_SUM : at + N_G + (i + 1) * N_SUM] for i in range(4)]
    tables = (user_tile, word_tile, subreddit)
    here = place()
    c, p, q, z = here
    fetches = [pltpu.make_async_copy(given[i], inputs[i], fetch_sems.at[i]) for i in range(10)]
    for fetch in fetches:
        fetch.start()
    for fetch in fetches[:2]:
        fetch.wait()
    padded = jnp.concatenate([activity[...], jnp.zeros((1, R - ROWS), F32)], axis=1)
    scales[q, z] = jnp.broadcast_to(padded, (8, R))
    enter(here)
    for fetch in fetches[2:9]:
        fetch.wait()

    def blocks(whole, values):
        rest = (whole, words, wide, tables, mask, values, part)
        middle, end = GROUPS // 4, GROUPS // 2
        block_sums(lambda n: 1 - c, 0, middle, *rest)
        core = to_partner(here, part, scatter[0], core_sem, 0)
        first = FirstRing(here, part, core, scatter, 0)
        block_sums(lambda n: c + (1 - 2 * c) * (n // middle), 0, end, *rest)
        core = to_partner(here, part, scatter[0], core_sem, 1)
        second = FirstRing(here, part, core, scatter, 1)
        first.start()
        block_sums(lambda n: c, middle, end, *rest)
        first.pass_on()
        second.start()
        second.pass_on()
        return first, second

    cuts = (0, 11, 22, GROUPS)

    def meanwhile(i):
        if i == 0:
            widen(subs, wide)
        masks(runs, counts, mask, cuts[i], cuts[i + 1])

    gather(here, start[...], whole0, gather_sems, scales=scales, scale_sems=scale_sems, meanwhile=meanwhile)
    columns_of(scales, scale)
    fetches[9].wait()
    core = blocks(whole0, held)
    scaled = scale[q, z]
    r = scaled * reduce_scatter(here, part, core, scatter) - RIDGE * start[...]
    norm = Sum(here, sums[0])
    gather(here, r, whole1, gather_sems, norm, folded(r * r))

    core = blocks(whole1, None)
    rr = norm.close()
    along = Sum(here, sums[1])
    rows = reduce_scatter(
        here, part, core, scatter, along, lambda qq: scale[qq] * whole1[c, p, qq].astype(F32), RIDGE * folded(r * r)
    )
    image = scaled * rows + RIDGE * r
    step = rr / along.close()
    solution = start[...] + step * r
    later = r - step * image
    norm = Sum(here, sums[2])
    gather(here, later, whole2, gather_sems, norm, folded(later * later))

    core = blocks(whole2, None)
    new = norm.close()
    ratio = new / rr
    d = later + ratio * r

    def weigh(qq):
        return scale[qq] * (whole2[c, p, qq].astype(F32) + ratio[:, :, None] * whole1[c, p, qq].astype(F32))

    along = Sum(here, sums[3])
    rest = RIDGE * later + ratio * image
    rows = reduce_scatter(here, part, core, scatter, along, weigh, folded(d * rest))
    step = new / along.close()
    out[...] = solution + step * d
    left[...] = later - step * (scaled * rows + rest)


def on_device(
    factor_start,
    activity,
    word_factors,
    sub_factors,
    ratings,
    user_tile,
    word_tile,
    subreddit,
    counts,
    runs,
):
    block = jax.ShapeDtypeStruct((ROWS, R), F32)
    return tuple(
        pl.pallas_call(
            step_kernel,
            out_shape=[block, block],
            in_specs=[pl.BlockSpec(memory_space=pl.ANY)] * 10,
            out_specs=[VMEM] * 2,
            scratch_shapes=INPUTS + SCRATCH + SCATTER_SCRATCH + GATHER_SCRATCH + SUM_SCRATCH * 4,
            compiler_params=pltpu.CompilerParams(
                collective_id=0, has_side_effects=True, vmem_limit_bytes=60 * 1024 * 1024
            ),
            name="step",
        )(
            factor_start,
            activity.reshape(1, ROWS),
            word_factors[0],
            sub_factors,
            runs[0, 0],
            counts[0, 0],
            user_tile[0, 0].T,
            word_tile[0, 0].T,
            subreddit[0, 0].T,
            ratings[0, 0],
        )
    )


def solution(mesh):
    placed = (
        P(("loop", "own"), None),
        P(("loop", "own")),
        P("loop", None, None, None),
        P(),
        P("loop", "own", None, None, None, None),
        P("loop", "own", None, None),
        P("loop", "own", None, None),
        P("loop", "own", None, None),
        P("loop", "own", None),
        P("loop", "own", None, None, None, None),
    )
    return jax.shard_map(
        on_device,
        mesh=mesh,
        in_specs=placed,
        out_specs=(P(("loop", "own"), None), P(("loop", "own"), None)),
        check_vma=False,
    )
```
